32 devices in a mesh: seq: 8 (over y, x, core), head: 4 (over z).
Axes of the slice: x: 2, y: 2, z: 4, core: 2. Of those that a mesh axis runs over, the one named last changes fastest.
Arguments:
- query_rows: bfloat16 [2048, 3072], P('seq', 'head'), may hold values from -60 to 60
- key_rows: bfloat16 [2048, 3072], P('seq', 'head'), may hold values from -5 to 5
- value_rows: bfloat16 [2048, 3072], P('seq', 'head'), may hold values from -6 to 6
- grad_out: bfloat16 [2048, 3072], P('seq', 'head'), may hold values from -6 to 6
Outputs:
- attended: bfloat16 [2048, 3072], P('seq', 'head')
- grad_query: bfloat16 [2048, 3072], P('seq', 'head')
- grad_keys: bfloat16 [2048, 3072], P('seq', 'head')
- grad_values: bfloat16 [2048, 3072], P('seq', 'head')
The draws below stay inside these ranges and needn't reach their ends.
All inputs are finite; a program needn't handle non-finite values.
Results may differ from the reference program's by a relative error of at most 0.0081.
Values may be sent and summed in bfloat16 or wider, within the bound.
A program may use at most 64 MiB of HBM per device.

```python
import jax
import jax.numpy as jnp
from jax import lax

HEADS = 24
HEAD_DIM = 128
BLOCK = 128
STRIDE = 512
SEQ_LEN = 2048


def shared_draw(key):
    base_key = jax.random.fold_in(key, 11)
    key_part, query_part = jax.random.split(base_key, 2)
    columns = HEADS * HEAD_DIM
    key_rows = jnp.clip(jax.random.normal(key_part, (SEQ_LEN, columns), jnp.float32), -5.0, 5.0)
    query_rows = jnp.clip(jax.random.normal(query_part, (SEQ_LEN, columns), jnp.float32), -5.0, 5.0)
    return (query_rows.astype(jnp.bfloat16), key_rows.astype(jnp.bfloat16))


def draw_query_rows(key, part):
    return shared_draw(key)[0]


def draw_key_rows(key, part):
    return shared_draw(key)[1]


def shard_levels(own_key, shape, pieces, low, top_value):
    loudness, own = 1.0, jax.random.fold_in(own_key, 6)
    for dim, blocks in pieces:
        steps = jnp.exp(jax.random.uniform(jax.random.fold_in(own, dim), (blocks,), jnp.float32, low / len(pieces), top_value / len(pieces)))
        loudness = loudness * jnp.repeat(steps, shape[dim] // blocks).reshape([-1 if axis == dim else 1 for axis in range(len(shape))])
    return loudness


def bell_draw(rng, dims, scale, limit, pieces=(), kind=jnp.bfloat16):
    array = scale * jax.random.normal(rng, dims, jnp.float32)
    if pieces:
        array = array * shard_levels(rng, dims, pieces, -0.22, 0.18)
    return jnp.clip(array, -limit, limit).astype(kind)


def setup_inputs(seed: int = 0) -> dict:
    arg_keys = jax.random.split(jax.random.key(seed), 5)
    query_rows = draw_query_rows(jax.random.fold_in(arg_keys[4], 71), 0)
    key_rows = draw_key_rows(jax.random.fold_in(arg_keys[4], 71), 0)
    value_rows = bell_draw(arg_keys[2], (SEQ_LEN, HEADS * HEAD_DIM), 1.0, 6.0, ((0, 8), (1, 4)))
    grad_out = bell_draw(arg_keys[3], (SEQ_LEN, HEADS * HEAD_DIM), 1.0, 6.0, ((0, 8), (1, 4)))
    return dict(query_rows=query_rows, key_rows=key_rows, value_rows=value_rows, grad_out=grad_out)


NEG_FILL = -1e30


def rounded(tensor):
    return lax.optimization_barrier(tensor.astype(jnp.bfloat16)).astype(jnp.float32)


def attend(queries, keyset, valueset, upstream, allowed, score_scale):
    scores = jnp.einsum('...qd,...kd->...qk', queries, keyset) * score_scale
    scores = jnp.where(allowed, scores, NEG_FILL)
    row_peak = jnp.max(scores, axis=-1, keepdims=True)
    log_total = row_peak + jnp.log(jnp.sum(jnp.exp(scores - row_peak), axis=-1, keepdims=True))
    weights = jnp.exp(scores - log_total)
    rounded_weights = rounded(weights)
    attended = jnp.einsum('...qk,...kd->...qd', rounded_weights, valueset).astype(jnp.bfloat16)
    out_float = lax.optimization_barrier(attended).astype(jnp.float32)
    row_dots = jnp.sum(upstream * out_float, axis=-1, keepdims=True)
    weight_grads = jnp.einsum('...qd,...kd->...qk', upstream, valueset)
    score_grads = rounded(weights * (weight_grads - row_dots))
    grad_query = (jnp.einsum('...qk,...kd->...qd', score_grads, keyset) * score_scale).astype(jnp.bfloat16)
    grad_keys = jnp.einsum('...qk,...qd->...kd', score_grads, queries) * score_scale
    grad_values = jnp.einsum('...qk,...qd->...kd', rounded_weights, upstream)
    return attended, grad_query, grad_keys, grad_values


def band_head(columns):
    block_count = SEQ_LEN // BLOCK
    queries, keyset, valueset, upstream = [tensor.astype(jnp.float32) for tensor in columns]

    def windowed(column):
        padded = jnp.concatenate([jnp.zeros((BLOCK, HEAD_DIM), jnp.float32), column], 0)
        padded = padded.reshape(block_count + 1, BLOCK, HEAD_DIM)
        return jnp.concatenate([padded[:-1], padded[1:]], 1)

    row_pos = jnp.arange(BLOCK)[:, None]
    key_pos = jnp.arange(2 * BLOCK)[None, :]
    block_pos = jnp.arange(block_count)[:, None, None]
    allowed = (key_pos > row_pos) & (key_pos <= row_pos + BLOCK) & ((block_pos - 1) * BLOCK + key_pos >= 0)
    attended, grad_query, key_terms, value_terms = attend(
        queries.reshape(block_count, BLOCK, HEAD_DIM), windowed(keyset), windowed(valueset),
        upstream.reshape(block_count, BLOCK, HEAD_DIM), allowed, HEAD_DIM ** -0.5)

    def folded(term_sums):
        zero_block = jnp.zeros((1, BLOCK, HEAD_DIM), jnp.float32)
        folded_sum = jnp.concatenate([term_sums[:, :BLOCK], zero_block], 0) + jnp.concatenate([zero_block, term_sums[:, BLOCK:]], 0)
        return folded_sum[1:].reshape(SEQ_LEN, HEAD_DIM).astype(jnp.bfloat16)

    return (attended.reshape(SEQ_LEN, HEAD_DIM), grad_query.reshape(SEQ_LEN, HEAD_DIM), folded(key_terms), folded(value_terms))


def strided_head(columns):
    group_span = SEQ_LEN // STRIDE

    def regroup(tensor):
        return jnp.transpose(tensor.astype(jnp.float32).reshape(group_span, STRIDE, HEAD_DIM), (1, 0, 2))

    def restore(tensor):
        return jnp.transpose(tensor, (1, 0, 2)).reshape(SEQ_LEN, HEAD_DIM).astype(jnp.bfloat16)

    causal_mask = jnp.arange(group_span)[None, :] <= jnp.arange(group_span)[:, None]
    results = attend(regroup(columns[0]), regroup(columns[1]), regroup(columns[2]), regroup(columns[3]), causal_mask, HEAD_DIM ** -0.5)
    return tuple(restore(tensor) for tensor in results)


def reference(query_rows, key_rows, value_rows, grad_out):
    inputs = (query_rows, key_rows, value_rows, grad_out)
    stride_offset = (HEADS // 2) * HEAD_DIM

    def one_pair(pair_index):
        column_start = pair_index * HEAD_DIM
        band_cols = tuple(lax.dynamic_slice_in_dim(tensor, column_start, HEAD_DIM, 1) for tensor in inputs)
        stride_cols = tuple(lax.dynamic_slice_in_dim(tensor, column_start + stride_offset, HEAD_DIM, 1) for tensor in inputs)
        return band_head(band_cols) + strided_head(stride_cols)

    results = lax.map(one_pair, jnp.arange(HEADS // 2, dtype=jnp.int32))
    outputs = []
    for slot in range(4):
        joined = jnp.concatenate([results[slot], results[slot + 4]], 0)
        outputs.append(jnp.transpose(joined, (1, 0, 2)).reshape(SEQ_LEN, HEADS * HEAD_DIM))
    return (outputs[0], outputs[1], outputs[2], outputs[3])
```

```python
import functools

import jax
import jax.numpy as jnp
from jax import lax
from jax.experimental import pallas as pl
from jax.experimental.pallas import tpu as pltpu
from jax.sharding import PartitionSpec as P

HEAD_DIM = 128
BLOCK = 128
STRIDE = 512


NEG_FILL = -1e30


def swapped(value, axis, stride):
    mask = 2**stride
    pairs = [(source, source ^ mask) for source in range(lax.axis_size(axis))]
    return lax.ppermute(value, axis, pairs)


def passed_along(shard, axis, by):
    size = lax.axis_size(axis)
    pairs = [(i, i + by) for i in range(size) if 0 <= i + by < size]
    return lax.ppermute(shard, axis, pairs)


def attend(queries, keyset, valueset, upstream, allowed, score_scale):
    scores = (
        jnp.einsum("...qd,...kd->...qk", queries, keyset, preferred_element_type=jnp.float32)
        * score_scale
    )
    scores = jnp.where(allowed, scores, NEG_FILL)
    row_peak = jnp.max(scores, axis=-1, keepdims=True)
    log_total = row_peak + jnp.log(jnp.sum(jnp.exp(scores - row_peak), axis=-1, keepdims=True))
    weights = jnp.exp(scores - log_total)
    rounded_weights = weights.astype(jnp.bfloat16)
    attended = jnp.einsum(
        "...qk,...kd->...qd", rounded_weights, valueset, preferred_element_type=jnp.float32
    ).astype(jnp.bfloat16)
    if upstream is None:
        return attended
    out_float = lax.optimization_barrier(attended).astype(jnp.float32)
    row_dots = jnp.sum(upstream.astype(jnp.float32) * out_float, axis=-1, keepdims=True)
    weight_grads = jnp.einsum(
        "...qd,...kd->...qk", upstream, valueset, preferred_element_type=jnp.float32
    )
    score_grads = (weights * (weight_grads - row_dots)).astype(jnp.bfloat16)
    grad_query = (
        jnp.einsum("...qk,...kd->...qd", score_grads, keyset, preferred_element_type=jnp.float32)
        * score_scale
    ).astype(jnp.bfloat16)
    grad_keys = (
        jnp.einsum("...qk,...qd->...kd", score_grads, queries, preferred_element_type=jnp.float32)
        * score_scale
    )
    grad_values = jnp.einsum(
        "...qk,...qd->...kd", rounded_weights, upstream, preferred_element_type=jnp.float32
    )
    return (attended, grad_query, grad_keys, grad_values)


def swapped_shards(query_rows, key_rows, value_rows, grad_out):
    local_rows, full_width = query_rows.shape
    half_heads = full_width // (2 * HEAD_DIM)
    score_scale = HEAD_DIM ** (-0.5)
    head_count = lax.axis_size("head")
    pair_bit = head_count.bit_length() - 2
    band_holder = lax.axis_index("head") < head_count // 2

    def halves(tensor):
        return tensor.reshape(local_rows, 2, half_heads, HEAD_DIM)

    split_in = [halves(tensor) for tensor in (query_rows, key_rows, value_rows, grad_out)]
    outgoing = [jnp.where(band_holder, tensor[:, 1], tensor[:, 0]) for tensor in split_in]
    staying = [jnp.where(band_holder, tensor[:, 0], tensor[:, 1]) for tensor in split_in]
    incoming = swapped((outgoing[0], outgoing[1], outgoing[2], outgoing[3]), "head", pair_bit)
    band_in = [
        jnp.where(band_holder, own_part, other_part)
        for own_part, other_part in zip(staying, incoming)
    ]
    stride_in = [
        jnp.where(band_holder, other_part, own_part)
        for own_part, other_part in zip(staying, incoming)
    ]
    block_count = local_rows // BLOCK
    band_query, band_keys, band_values, band_grads = band_in
    before_rows = passed_along(
        (band_keys[local_rows - BLOCK :], band_values[local_rows - BLOCK :]), "seq", 1
    )

    def blocked(tensor):
        return jnp.swapaxes(tensor.reshape(block_count, BLOCK, half_heads, HEAD_DIM), 1, 2)

    def windowed(earlier, tensor):
        joined = jnp.concatenate([earlier, tensor], 0).reshape(
            block_count + 1, BLOCK, half_heads, HEAD_DIM
        )
        return jnp.swapaxes(jnp.concatenate([joined[:-1], joined[1:]], 1), 1, 2)

    anchor = lax.axis_index("seq") * local_rows
    row_pos = jnp.arange(BLOCK)[:, None]
    key_pos = jnp.arange(2 * BLOCK)[None, :]
    block_pos = jnp.arange(block_count)[:, None, None, None]
    allowed = (
        (key_pos > row_pos)
        & (key_pos <= row_pos + BLOCK)
        & (anchor + (block_pos - 1) * BLOCK + key_pos >= 0)
    )
    band_out, band_dq, key_terms, value_terms = attend(
        blocked(band_query),
        windowed(before_rows[0], band_keys),
        windowed(before_rows[1], band_values),
        blocked(band_grads),
        allowed,
        score_scale,
    )

    def unblocked(tensor):
        return jnp.swapaxes(tensor, 1, 2).reshape(local_rows, half_heads, HEAD_DIM)

    def folded(term_sums):
        spread = jnp.swapaxes(term_sums, 1, 2)
        zero_block = jnp.zeros((1, BLOCK, half_heads, HEAD_DIM), jnp.float32)
        return jnp.concatenate([spread[:, :BLOCK], zero_block], 0) + jnp.concatenate(
            [zero_block, spread[:, BLOCK:]], 0
        )

    key_total = folded(key_terms)
    value_total = folded(value_terms)
    after_terms = (
        passed_along(key_total[0].astype(jnp.bfloat16), "seq", -1).astype(jnp.float32),
        passed_along(value_total[0].astype(jnp.bfloat16), "seq", -1).astype(jnp.float32),
    )
    band_dk = (
        key_total[1:]
        .at[block_count - 1]
        .add(after_terms[0])
        .reshape(local_rows, half_heads, HEAD_DIM)
        .astype(jnp.bfloat16)
    )
    band_dv = (
        value_total[1:]
        .at[block_count - 1]
        .add(after_terms[1])
        .reshape(local_rows, half_heads, HEAD_DIM)
        .astype(jnp.bfloat16)
    )
    band_results = (unblocked(band_out), unblocked(band_dq), band_dk, band_dv)
    seq_count = lax.axis_size("seq")
    group_count = STRIDE // seq_count
    group_span = local_rows // group_count

    def offset_in(tensor):
        return tensor.reshape(local_rows // seq_count, seq_count, half_heads, HEAD_DIM)

    def regroup(tensor):
        return jnp.transpose(
            tensor.reshape(group_span, group_count, tensor.shape[2], HEAD_DIM), (1, 2, 0, 3)
        )

    def restore(tensor):
        return jnp.transpose(tensor, (2, 0, 1, 3)).reshape(local_rows, 1, tensor.shape[1], HEAD_DIM)

    causal_mask = jnp.arange(group_span)[None, :] <= jnp.arange(group_span)[:, None]
    stride_query, stride_keys, stride_values, stride_grads = [
        offset_in(tensor) for tensor in stride_in
    ]
    pieces = (
        lax.all_to_all(stride_query, "seq", split_axis=1, concat_axis=0, tiled=True),
        lax.all_to_all(stride_keys, "seq", split_axis=1, concat_axis=0, tiled=True),
        lax.all_to_all(stride_values, "seq", split_axis=1, concat_axis=0, tiled=True),
    )
    attended = attend(
        regroup(pieces[0]), regroup(pieces[1]), regroup(pieces[2]), None, causal_mask, score_scale
    )
    stride_out = lax.all_to_all(restore(attended), "seq", split_axis=0, concat_axis=1, tiled=True)
    pieces = (
        lax.all_to_all(stride_query, "seq", split_axis=1, concat_axis=0, tiled=True),
        lax.all_to_all(stride_keys, "seq", split_axis=1, concat_axis=0, tiled=True),
        lax.all_to_all(stride_values, "seq", split_axis=1, concat_axis=0, tiled=True),
        lax.all_to_all(stride_grads, "seq", split_axis=1, concat_axis=0, tiled=True),
    )
    results = attend(
        regroup(pieces[0]),
        regroup(pieces[1]),
        regroup(pieces[2]),
        regroup(pieces[3]),
        causal_mask,
        score_scale,
    )
    stride_dq = lax.all_to_all(restore(results[1]), "seq", split_axis=0, concat_axis=1, tiled=True)
    stride_dk = lax.all_to_all(
        restore(results[2].astype(jnp.bfloat16)), "seq", split_axis=0, concat_axis=1, tiled=True
    )
    stride_dv = lax.all_to_all(
        restore(results[3].astype(jnp.bfloat16)), "seq", split_axis=0, concat_axis=1, tiled=True
    )
    stride_results = tuple(
        (
            tensor.reshape(local_rows, half_heads, HEAD_DIM)
            for tensor in (stride_out, stride_dq, stride_dk, stride_dv)
        )
    )
    send_back = [
        jnp.where(band_holder, stride_part, band_part)
        for band_part, stride_part in zip(band_results, stride_results)
    ]
    keep_back = [
        jnp.where(band_holder, band_part, stride_part)
        for band_part, stride_part in zip(band_results, stride_results)
    ]
    returned = swapped((send_back[0], send_back[1], send_back[2], send_back[3]), "head", pair_bit)
    outputs = []
    for kept_part, got_part in zip(keep_back, returned):
        first_half = jnp.where(band_holder, kept_part, got_part)
        second_half = jnp.where(band_holder, got_part, kept_part)
        outputs.append(jnp.stack([first_half, second_half], 1).reshape(local_rows, full_width))
    return (outputs[0], outputs[1], outputs[2], outputs[3])


MESH = pl.DeviceIdType.MESH
CHUNK_HEADS = 2
ROW_TILE = 16


def lane_dot(left, right):
    return jnp.sum(left * right, axis=-1, keepdims=True)


def as_bf16(tensor):
    return tensor.astype(jnp.bfloat16).astype(jnp.float32)


def strided_tile(span, score_scale, queries, keyset, valueset, upstream):
    attended, grad_query = [None] * span, [None] * span
    grad_keys, grad_values = [None] * span, [None] * span

    def plus(total, term):
        return term if total is None else total + term

    for p in range(span):
        scores = [lane_dot(queries[p], keyset[j]) * score_scale for j in range(p + 1)]
        peak = functools.reduce(jnp.maximum, scores)
        total = functools.reduce(jnp.add, [jnp.exp(score - peak) for score in scores])
        log_total = peak + jnp.log(total)
        weights = [jnp.exp(score - log_total) for score in scores]
        rounded_weights = [as_bf16(weight) for weight in weights]
        out = None
        for j in range(p + 1):
            out = plus(out, rounded_weights[j] * valueset[j])
            grad_values[j] = plus(grad_values[j], rounded_weights[j] * upstream[p])
        attended[p] = out.astype(jnp.bfloat16)
        row_dots = lane_dot(upstream[p], attended[p].astype(jnp.float32))
        dq = None
        for j in range(p + 1):
            weight_grads = lane_dot(upstream[p], valueset[j])
            score_grads = as_bf16(weights[j] * (weight_grads - row_dots))
            dq = plus(dq, score_grads * keyset[j])
            grad_keys[j] = plus(grad_keys[j], score_grads * queries[p])
        grad_query[p] = dq * score_scale
    grad_keys = [tensor * score_scale for tensor in grad_keys]
    return attended, grad_query, grad_keys, grad_values


def strided_role(span, hop, ins, outs, gathered, results, sems):
    in_send, in_recv, out_send, out_recv, own_sem = sems
    rows, width = ins[0].shape
    piece = rows // span
    slab = lax.axis_index("seq")
    place = slab // hop
    offset = lax.rem(slab, hop)
    chunk_cols = CHUNK_HEADS * HEAD_DIM
    chunks = width // chunk_cols
    score_scale = HEAD_DIM ** (-0.5)

    def partner(step):
        return lax.rem(place + step, span)

    def seq_of(member):
        return {"seq": member * hop + offset}

    barrier = pltpu.get_barrier_semaphore()
    for step in range(1, span):
        pl.semaphore_signal(barrier, 1, device_id=seq_of(partner(step)), device_id_type=MESH)
    pl.semaphore_wait(barrier, span - 1)

    def piece_rows(member):
        return pl.ds(pl.multiple_of(member * piece, piece), piece)

    own = []
    for i in range(4):
        copy = pltpu.make_async_copy(
            ins[i].at[piece_rows(place)], gathered.at[i, place], own_sem.at[i]
        )
        copy.start()
        own.append(copy)
    incoming = []
    for c in range(chunks):
        cols = pl.ds(c * chunk_cols, chunk_cols)
        copies = []
        for step in range(1, span):
            member = partner(step)
            for i in range(4):
                copy = pltpu.make_async_remote_copy(
                    src_ref=ins[i].at[piece_rows(member), cols],
                    dst_ref=gathered.at[i, place, :, cols],
                    send_sem=in_send.at[c, step - 1, i],
                    recv_sem=in_recv.at[c, step - 1, i],
                    device_id=seq_of(member),
                    device_id_type=MESH,
                )
                copy.start()
                copies.append(copy)
        incoming.append(copies)
    for copy in own:
        copy.wait()
    outgoing = []
    tiles = piece // ROW_TILE
    for c in range(chunks):
        for copy in incoming[c]:
            copy.wait_recv()

        def body(index, carry, c=c):
            row = pl.ds(pl.multiple_of(lax.rem(index, tiles) * ROW_TILE, ROW_TILE), ROW_TILE)
            col = pl.ds(
                pl.multiple_of(c * chunk_cols + (index // tiles) * HEAD_DIM, HEAD_DIM), HEAD_DIM
            )
            loaded = [
                [gathered[i, j, row, col].astype(jnp.float32) for j in range(span)]
                for i in range(4)
            ]
            made = strided_tile(span, score_scale, *loaded)
            for i in range(4):
                for j in range(span):
                    results[i, j, row, col] = made[i][j].astype(jnp.bfloat16)
            return carry

        lax.fori_loop(0, tiles * CHUNK_HEADS, body, 0)
        cols = pl.ds(c * chunk_cols, chunk_cols)
        for step in range(1, span):
            member = partner(step)
            for i in range(4):
                copy = pltpu.make_async_remote_copy(
                    src_ref=results.at[i, member, :, cols],
                    dst_ref=outs[i].at[piece_rows(place), cols],
                    send_sem=out_send.at[c, step - 1, i],
                    recv_sem=out_recv.at[c, step - 1, i],
                    device_id=seq_of(member),
                    device_id_type=MESH,
                )
                copy.start()
                outgoing.append(copy)
    for i in range(4):
        outs[i][piece_rows(place), :] = results[i, place]
    for copies in incoming:
        for copy in copies:
            copy.wait_send()
    for copy in outgoing:
        copy.wait()


def dot_nt(left, right):
    return lax.dot_general(left, right, (((1,), (1,)), ((), ())), preferred_element_type=jnp.float32)


def dot_nn(left, right):
    return lax.dot_general(left, right, (((1,), (0,)), ((), ())), preferred_element_type=jnp.float32)


def dot_tn(left, right):
    return lax.dot_general(left, right, (((0,), (0,)), ((), ())), preferred_element_type=jnp.float32)


def band_role(ins, outs, halo, held, terms, after, sems):
    halo_send, halo_recv, after_send, after_recv = sems
    query_ref, key_ref, value_ref, grad_ref = ins
    out_ref, dq_ref, dk_ref, dv_ref = outs
    rows, width = query_ref.shape
    heads = width // HEAD_DIM
    blocks = rows // BLOCK
    slab = lax.axis_index("seq")
    slabs = lax.axis_size("seq")
    has_before = slab > 0
    has_after = slab < slabs - 1
    score_scale = HEAD_DIM ** (-0.5)
    before_id = {"seq": jnp.maximum(slab - 1, 0)}
    after_id = {"seq": jnp.minimum(slab + 1, slabs - 1)}

    barrier = pltpu.get_barrier_semaphore()

    @pl.when(has_before)
    def _():
        pl.semaphore_signal(barrier, 1, device_id=before_id, device_id_type=MESH)

    @pl.when(has_after)
    def _():
        pl.semaphore_signal(barrier, 1, device_id=after_id, device_id_type=MESH)

    peers = has_before.astype(jnp.int32) + has_after.astype(jnp.int32)
    pl.semaphore_wait(barrier, peers)

    last_rows = pl.ds(rows - BLOCK, BLOCK)
    halo_copies = [
        pltpu.make_async_remote_copy(
            src_ref=ref.at[last_rows],
            dst_ref=halo.at[i],
            send_sem=halo_send.at[i],
            recv_sem=halo_recv.at[i],
            device_id=after_id,
            device_id_type=MESH,
        )
        for i, ref in enumerate((key_ref, value_ref))
    ]
    after_copies = [
        pltpu.make_async_remote_copy(
            src_ref=terms.at[i],
            dst_ref=after.at[i],
            send_sem=after_send.at[i],
            recv_sem=after_recv.at[i],
            device_id=before_id,
            device_id_type=MESH,
        )
        for i in range(2)
    ]

    @pl.when(has_after)
    def _():
        for copy in halo_copies:
            copy.start()

    row_pos = lax.broadcasted_iota(jnp.int32, (BLOCK, 2 * BLOCK), 0)
    key_pos = lax.broadcasted_iota(jnp.int32, (BLOCK, 2 * BLOCK), 1)
    in_window = (key_pos > row_pos) & (key_pos <= row_pos + BLOCK)
    in_first = in_window & (slab * rows - BLOCK + key_pos >= 0)

    def block_step(block, allowed, h):
        col = pl.ds(pl.multiple_of(h * HEAD_DIM, HEAD_DIM), HEAD_DIM)
        own = pl.ds(block * BLOCK, BLOCK)
        prev = pl.ds((block - 1) * BLOCK, BLOCK)
        if block == 0:
            before_keys, before_values = halo[0, :, col], halo[1, :, col]
        else:
            before_keys, before_values = key_ref[prev, col], value_ref[prev, col]
        keyset = jnp.concatenate([before_keys, key_ref[own, col]], 0)
        valueset = jnp.concatenate([before_values, value_ref[own, col]], 0)
        queries, upstream = query_ref[own, col], grad_ref[own, col]
        scores = jnp.where(allowed, dot_nt(queries, keyset) * score_scale, NEG_FILL)
        peak = jnp.max(scores, axis=-1, keepdims=True)
        log_total = peak + jnp.log(jnp.sum(jnp.exp(scores - peak), axis=-1, keepdims=True))
        weights = jnp.exp(scores - log_total)
        rounded_weights = weights.astype(jnp.bfloat16)
        attended = dot_nn(rounded_weights, valueset).astype(jnp.bfloat16)
        row_dots = lane_dot(upstream.astype(jnp.float32), attended.astype(jnp.float32))
        weight_grads = dot_nt(upstream, valueset)
        score_grads = (weights * (weight_grads - row_dots)).astype(jnp.bfloat16)
        out_ref[own, col] = attended
        dq_ref[own, col] = (dot_nn(score_grads, keyset) * score_scale).astype(jnp.bfloat16)
        key_terms = dot_tn(score_grads, queries) * score_scale
        value_terms = dot_tn(rounded_weights, upstream)
        for i, sums in enumerate((key_terms, value_terms)):
            dst = (dk_ref, dv_ref)[i]
            if block == blocks - 1:
                held[i, block, :, col] = sums[BLOCK:]
            else:
                total = sums[BLOCK:] + held[i, block, :, col]
                dst[own, col] = total.astype(jnp.bfloat16)
            if block > 0:
                held[i, block - 1, :, col] = sums[:BLOCK]
            else:
                terms[i, :, col] = sums[:BLOCK].astype(jnp.bfloat16)

    for block in range(blocks - 1, 0, -1):

        def body(h, carry, block=block):
            block_step(block, in_window, h)
            return carry

        lax.fori_loop(0, heads, body, 0)

    @pl.when(has_before)
    def _():
        for copy in halo_copies:
            copy.wait_recv()

    @pl.when(jnp.logical_not(has_before))
    def _():
        halo[...] = jnp.zeros_like(halo)

    def first_body(h, carry):
        block_step(0, in_first, h)
        return carry

    lax.fori_loop(0, heads, first_body, 0)

    @pl.when(has_before)
    def _():
        for copy in after_copies:
            copy.start()

    @pl.when(has_after)
    def _():
        for copy in after_copies:
            copy.wait_recv()

    @pl.when(jnp.logical_not(has_after))
    def _():
        after[...] = jnp.zeros_like(after)

    for i, dst in enumerate((dk_ref, dv_ref)):
        dst[last_rows, :] = (held[i, blocks - 1] + after[i].astype(jnp.float32)).astype(
            jnp.bfloat16
        )

    @pl.when(has_before)
    def _():
        for copy in after_copies:
            copy.wait_send()

    @pl.when(has_after)
    def _():
        for copy in halo_copies:
            copy.wait_send()


def fused_kernel(span, hop, *refs):
    ins, outs = refs[:4], refs[4:8]
    gathered, results, halo, held, terms, after = refs[8:14]
    sems = refs[14:]
    is_band = lax.axis_index("head") < lax.axis_size("head") // 2

    @pl.when(is_band)
    def _():
        band_role(ins, outs, halo, held, terms, after, sems[5:])

    @pl.when(jnp.logical_not(is_band))
    def _():
        strided_role(span, hop, ins, outs, gathered, results, sems[:5])


def fused_shards(span, hop, *tensors):
    rows, width = tensors[0].shape
    piece = rows // span
    chunks = width // (CHUNK_HEADS * HEAD_DIM)
    copy_sems = pltpu.SemaphoreType.DMA((chunks, span - 1, 4))
    pair_sems = pltpu.SemaphoreType.DMA((2,))
    vmem = pl.BlockSpec(memory_space=pltpu.VMEM)
    return tuple(
        pl.pallas_call(
            functools.partial(fused_kernel, span, hop),
            out_shape=[jax.ShapeDtypeStruct((rows, width), jnp.bfloat16)] * 4,
            in_specs=[vmem] * 4,
            out_specs=[vmem] * 4,
            scratch_shapes=[
                pltpu.VMEM((4, span, piece, width), jnp.bfloat16),
                pltpu.VMEM((4, span, piece, width), jnp.bfloat16),
                pltpu.VMEM((2, BLOCK, width), jnp.bfloat16),
                pltpu.VMEM((2, rows // BLOCK, BLOCK, width), jnp.float32),
                pltpu.VMEM((2, BLOCK, width), jnp.bfloat16),
                pltpu.VMEM((2, BLOCK, width), jnp.bfloat16),
                copy_sems,
                copy_sems,
                copy_sems,
                copy_sems,
                pltpu.SemaphoreType.DMA((4,)),
                pair_sems,
                pair_sems,
                pair_sems,
                pair_sems,
            ],
            compiler_params=pltpu.CompilerParams(collective_id=0, has_side_effects=True),
        )(*tensors)
    )


def shards(query_rows, key_rows, value_rows, grad_out):
    rows = query_rows.shape[0]
    hop = STRIDE // rows
    span = lax.axis_size("seq") // hop
    if span <= 8 and rows % (span * ROW_TILE) == 0:
        return fused_shards(span, hop, query_rows, key_rows, value_rows, grad_out)
    return swapped_shards(query_rows, key_rows, value_rows, grad_out)


def solution(mesh):
    return jax.shard_map(
        shards,
        mesh=mesh,
        in_specs=(P("seq", "head"), P("seq", "head"), P("seq", "head"), P("seq", "head")),
        out_specs=(P("seq", "head"), P("seq", "head"), P("seq", "head"), P("seq", "head")),
        check_vma=False,
    )
```

```python
import functools

import jax
import jax.numpy as jnp
from jax import lax
from jax.experimental import pallas as pl
from jax.experimental.pallas import tpu as pltpu
from jax.sharding import PartitionSpec as P

HEAD_DIM = 128
BLOCK = 128
STRIDE = 512


NEG_FILL = -1e30


def swapped(value, axis, stride):
    mask = 2**stride
    pairs = [(source, source ^ mask) for source in range(lax.axis_size(axis))]
    return lax.ppermute(value, axis, pairs)


def passed_along(shard, axis, by):
    size = lax.axis_size(axis)
    pairs = [(i, i + by) for i in range(size) if 0 <= i + by < size]
    return lax.ppermute(shard, axis, pairs)


def attend(queries, keyset, valueset, upstream, allowed, score_scale):
    scores = (
        jnp.einsum("...qd,...kd->...qk", queries, keyset, preferred_element_type=jnp.float32)
        * score_scale
    )
    scores = jnp.where(allowed, scores, NEG_FILL)
    row_peak = jnp.max(scores, axis=-1, keepdims=True)
    log_total = row_peak + jnp.log(jnp.sum(jnp.exp(scores - row_peak), axis=-1, keepdims=True))
    weights = jnp.exp(scores - log_total)
    rounded_weights = weights.astype(jnp.bfloat16)
    attended = jnp.einsum(
        "...qk,...kd->...qd", rounded_weights, valueset, preferred_element_type=jnp.float32
    ).astype(jnp.bfloat16)
    if upstream is None:
        return attended
    out_float = lax.optimization_barrier(attended).astype(jnp.float32)
    row_dots = jnp.sum(upstream.astype(jnp.float32) * out_float, axis=-1, keepdims=True)
    weight_grads = jnp.einsum(
        "...qd,...kd->...qk", upstream, valueset, preferred_element_type=jnp.float32
    )
    score_grads = (weights * (weight_grads - row_dots)).astype(jnp.bfloat16)
    grad_query = (
        jnp.einsum("...qk,...kd->...qd", score_grads, keyset, preferred_element_type=jnp.float32)
        * score_scale
    ).astype(jnp.bfloat16)
    grad_keys = (
        jnp.einsum("...qk,...qd->...kd", score_grads, queries, preferred_element_type=jnp.float32)
        * score_scale
    )
    grad_values = jnp.einsum(
        "...qk,...qd->...kd", rounded_weights, upstream, preferred_element_type=jnp.float32
    )
    return (attended, grad_query, grad_keys, grad_values)


def swapped_shards(query_rows, key_rows, value_rows, grad_out):
    local_rows, full_width = query_rows.shape
    half_heads = full_width // (2 * HEAD_DIM)
    score_scale = HEAD_DIM ** (-0.5)
    head_count = lax.axis_size("head")
    pair_bit = head_count.bit_length() - 2
    band_holder = lax.axis_index("head") < head_count // 2

    def halves(tensor):
        return tensor.reshape(local_rows, 2, half_heads, HEAD_DIM)

    split_in = [halves(tensor) for tensor in (query_rows, key_rows, value_rows, grad_out)]
    outgoing = [jnp.where(band_holder, tensor[:, 1], tensor[:, 0]) for tensor in split_in]
    staying = [jnp.where(band_holder, tensor[:, 0], tensor[:, 1]) for tensor in split_in]
    incoming = swapped((outgoing[0], outgoing[1], outgoing[2], outgoing[3]), "head", pair_bit)
    band_in = [
        jnp.where(band_holder, own_part, other_part)
        for own_part, other_part in zip(staying, incoming)
    ]
    stride_in = [
        jnp.where(band_holder, other_part, own_part)
        for own_part, other_part in zip(staying, incoming)
    ]
    block_count = local_rows // BLOCK
    band_query, band_keys, band_values, band_grads = band_in
    before_rows = passed_along(
        (band_keys[local_rows - BLOCK :], band_values[local_rows - BLOCK :]), "seq", 1
    )

    def blocked(tensor):
        return jnp.swapaxes(tensor.reshape(block_count, BLOCK, half_heads, HEAD_DIM), 1, 2)

    def windowed(earlier, tensor):
        joined = jnp.concatenate([earlier, tensor], 0).reshape(
            block_count + 1, BLOCK, half_heads, HEAD_DIM
        )
        return jnp.swapaxes(jnp.concatenate([joined[:-1], joined[1:]], 1), 1, 2)

    anchor = lax.axis_index("seq") * local_rows
    row_pos = jnp.arange(BLOCK)[:, None]
    key_pos = jnp.arange(2 * BLOCK)[None, :]
    block_pos = jnp.arange(block_count)[:, None, None, None]
    allowed = (
        (key_pos > row_pos)
        & (key_pos <= row_pos + BLOCK)
        & (anchor + (block_pos - 1) * BLOCK + key_pos >= 0)
    )
    band_out, band_dq, key_terms, value_terms = attend(
        blocked(band_query),
        windowed(before_rows[0], band_keys),
        windowed(before_rows[1], band_values),
        blocked(band_grads),
        allowed,
        score_scale,
    )

    def unblocked(tensor):
        return jnp.swapaxes(tensor, 1, 2).reshape(local_rows, half_heads, HEAD_DIM)

    def folded(term_sums):
        spread = jnp.swapaxes(term_sums, 1, 2)
        zero_block = jnp.zeros((1, BLOCK, half_heads, HEAD_DIM), jnp.float32)
        return jnp.concatenate([spread[:, :BLOCK], zero_block], 0) + jnp.concatenate(
            [zero_block, spread[:, BLOCK:]], 0
        )

    key_total = folded(key_terms)
    value_total = folded(value_terms)
    after_terms = (
        passed_along(key_total[0].astype(jnp.bfloat16), "seq", -1).astype(jnp.float32),
        passed_along(value_total[0].astype(jnp.bfloat16), "seq", -1).astype(jnp.float32),
    )
    band_dk = (
        key_total[1:]
        .at[block_count - 1]
        .add(after_terms[0])
        .reshape(local_rows, half_heads, HEAD_DIM)
        .astype(jnp.bfloat16)
    )
    band_dv = (
        value_total[1:]
        .at[block_count - 1]
        .add(after_terms[1])
        .reshape(local_rows, half_heads, HEAD_DIM)
        .astype(jnp.bfloat16)
    )
    band_results = (unblocked(band_out), unblocked(band_dq), band_dk, band_dv)
    seq_count = lax.axis_size("seq")
    group_count = STRIDE // seq_count
    group_span = local_rows // group_count

    def offset_in(tensor):
        return tensor.reshape(local_rows // seq_count, seq_count, half_heads, HEAD_DIM)

    def regroup(tensor):
        return jnp.transpose(
            tensor.reshape(group_span, group_count, tensor.shape[2], HEAD_DIM), (1, 2, 0, 3)
        )

    def restore(tensor):
        return jnp.transpose(tensor, (2, 0, 1, 3)).reshape(local_rows, 1, tensor.shape[1], HEAD_DIM)

    causal_mask = jnp.arange(group_span)[None, :] <= jnp.arange(group_span)[:, None]
    stride_query, stride_keys, stride_values, stride_grads = [
        offset_in(tensor) for tensor in stride_in
    ]
    pieces = (
        lax.all_to_all(stride_query, "seq", split_axis=1, concat_axis=0, tiled=True),
        lax.all_to_all(stride_keys, "seq", split_axis=1, concat_axis=0, tiled=True),
        lax.all_to_all(stride_values, "seq", split_axis=1, concat_axis=0, tiled=True),
    )
    attended = attend(
        regroup(pieces[0]), regroup(pieces[1]), regroup(pieces[2]), None, causal_mask, score_scale
    )
    stride_out = lax.all_to_all(restore(attended), "seq", split_axis=0, concat_axis=1, tiled=True)
    pieces = (
        lax.all_to_all(stride_query, "seq", split_axis=1, concat_axis=0, tiled=True),
        lax.all_to_all(stride_keys, "seq", split_axis=1, concat_axis=0, tiled=True),
        lax.all_to_all(stride_values, "seq", split_axis=1, concat_axis=0, tiled=True),
        lax.all_to_all(stride_grads, "seq", split_axis=1, concat_axis=0, tiled=True),
    )
    results = attend(
        regroup(pieces[0]),
        regroup(pieces[1]),
        regroup(pieces[2]),
        regroup(pieces[3]),
        causal_mask,
        score_scale,
    )
    stride_dq = lax.all_to_all(restore(results[1]), "seq", split_axis=0, concat_axis=1, tiled=True)
    stride_dk = lax.all_to_all(
        restore(results[2].astype(jnp.bfloat16)), "seq", split_axis=0, concat_axis=1, tiled=True
    )
    stride_dv = lax.all_to_all(
        restore(results[3].astype(jnp.bfloat16)), "seq", split_axis=0, concat_axis=1, tiled=True
    )
    stride_results = tuple(
        (
            tensor.reshape(local_rows, half_heads, HEAD_DIM)
            for tensor in (stride_out, stride_dq, stride_dk, stride_dv)
        )
    )
    send_back = [
        jnp.where(band_holder, stride_part, band_part)
        for band_part, stride_part in zip(band_results, stride_results)
    ]
    keep_back = [
        jnp.where(band_holder, band_part, stride_part)
        for band_part, stride_part in zip(band_results, stride_results)
    ]
    returned = swapped((send_back[0], send_back[1], send_back[2], send_back[3]), "head", pair_bit)
    outputs = []
    for kept_part, got_part in zip(keep_back, returned):
        first_half = jnp.where(band_holder, kept_part, got_part)
        second_half = jnp.where(band_holder, got_part, kept_part)
        outputs.append(jnp.stack([first_half, second_half], 1).reshape(local_rows, full_width))
    return (outputs[0], outputs[1], outputs[2], outputs[3])


MESH = pl.DeviceIdType.MESH
CHUNK_HEADS = 2
ROW_TILE = 16


def lane_dot(left, right):
    return jnp.sum(left * right, axis=-1, keepdims=True)


def as_bf16(tensor):
    return tensor.astype(jnp.bfloat16).astype(jnp.float32)


def strided_tile(span, score_scale, queries, keyset, valueset, upstream):
    attended, grad_query = [None] * span, [None] * span
    grad_keys, grad_values = [None] * span, [None] * span

    def plus(total, term):
        return term if total is None else total + term

    for p in range(span):
        scores = [lane_dot(queries[p], keyset[j]) * score_scale for j in range(p + 1)]
        peak = functools.reduce(jnp.maximum, scores)
        total = functools.reduce(jnp.add, [jnp.exp(score - peak) for score in scores])
        log_total = peak + jnp.log(total)
        weights = [jnp.exp(score - log_total) for score in scores]
        rounded_weights = [as_bf16(weight) for weight in weights]
        out = None
        for j in range(p + 1):
            out = plus(out, rounded_weights[j] * valueset[j])
            grad_values[j] = plus(grad_values[j], rounded_weights[j] * upstream[p])
        attended[p] = out.astype(jnp.bfloat16)
        row_dots = lane_dot(upstream[p], attended[p].astype(jnp.float32))
        dq = None
        for j in range(p + 1):
            weight_grads = lane_dot(upstream[p], valueset[j])
            score_grads = as_bf16(weights[j] * (weight_grads - row_dots))
            dq = plus(dq, score_grads * keyset[j])
            grad_keys[j] = plus(grad_keys[j], score_grads * queries[p])
        grad_query[p] = dq * score_scale
    grad_keys = [tensor * score_scale for tensor in grad_keys]
    return attended, grad_query, grad_keys, grad_values


def strided_role(span, hop, ins, outs, gathered, results, sems):
    in_send, in_recv, out_send, out_recv, own_sem = sems
    rows, width = ins[0].shape
    piece = rows // span
    slab = lax.axis_index("seq")
    place = slab // hop
    offset = lax.rem(slab, hop)
    chunk_cols = CHUNK_HEADS * HEAD_DIM
    chunks = width // chunk_cols
    score_scale = HEAD_DIM ** (-0.5)

    def partner(step):
        return lax.rem(place + step, span)

    def seq_of(member):
        return {"seq": member * hop + offset}

    barrier = pltpu.get_barrier_semaphore()
    for step in range(1, span):
        pl.semaphore_signal(barrier, 1, device_id=seq_of(partner(step)), device_id_type=MESH)
    pl.semaphore_wait(barrier, span - 1)

    def piece_rows(member):
        return pl.ds(pl.multiple_of(member * piece, piece), piece)

    own = []
    for i in range(4):
        copy = pltpu.make_async_copy(
            ins[i].at[piece_rows(place)], gathered.at[i, place], own_sem.at[i]
        )
        copy.start()
        own.append(copy)
    incoming = []
    for c in range(chunks):
        cols = pl.ds(c * chunk_cols, chunk_cols)
        copies = []
        for step in range(1, span):
            member = partner(step)
            for i in range(4):
                copy = pltpu.make_async_remote_copy(
                    src_ref=ins[i].at[piece_rows(member), cols],
                    dst_ref=gathered.at[i, place, :, cols],
                    send_sem=in_send.at[c, step - 1, i],
                    recv_sem=in_recv.at[c, step - 1, i],
                    device_id=seq_of(member),
                    device_id_type=MESH,
                )
                copy.start()
                copies.append(copy)
        incoming.append(copies)
    for copy in own:
        copy.wait()
    outgoing = []
    tiles = piece // ROW_TILE
    for c in range(chunks):
        for copy in incoming[c]:
            copy.wait_recv()

        def body(index, carry, c=c):
            row = pl.ds(pl.multiple_of(lax.rem(index, tiles) * ROW_TILE, ROW_TILE), ROW_TILE)
            col = pl.ds(
                pl.multiple_of(c * chunk_cols + (index // tiles) * HEAD_DIM, HEAD_DIM), HEAD_DIM
            )
            loaded = [
                [gathered[i, j, row, col].astype(jnp.float32) for j in range(span)]
                for i in range(4)
            ]
            made = strided_tile(span, score_scale, *loaded)
            for i in range(4):
                for j in range(span):
                    results[i, j, row, col] = made[i][j].astype(jnp.bfloat16)
            return carry

        lax.fori_loop(0, tiles * CHUNK_HEADS, body, 0)
        cols = pl.ds(c * chunk_cols, chunk_cols)
        for step in range(1, span):
            member = partner(step)
            for i in range(4):
                copy = pltpu.make_async_remote_copy(
                    src_ref=results.at[i, member, :, cols],
                    dst_ref=outs[i].at[piece_rows(place), cols],
                    send_sem=out_send.at[c, step - 1, i],
                    recv_sem=out_recv.at[c, step - 1, i],
                    device_id=seq_of(member),
                    device_id_type=MESH,
                )
                copy.start()
                outgoing.append(copy)
    for i in range(4):
        outs[i][piece_rows(place), :] = results[i, place]
    for copies in incoming:
        for copy in copies:
            copy.wait_send()
    for copy in outgoing:
        copy.wait()


def dot_nt(left, right):
    return lax.dot_general(left, right, (((1,), (1,)), ((), ())), preferred_element_type=jnp.float32)


def dot_nn(left, right):
    return lax.dot_general(left, right, (((1,), (0,)), ((), ())), preferred_element_type=jnp.float32)


def dot_tn(left, right):
    return lax.dot_general(left, right, (((0,), (0,)), ((), ())), preferred_element_type=jnp.float32)


def band_role(ins, outs, halo, held, terms, after, sems):
    halo_send, halo_recv, after_send, after_recv = sems
    query_ref, key_ref, value_ref, grad_ref = ins
    out_ref, dq_ref, dk_ref, dv_ref = outs
    rows, width = query_ref.shape
    heads = width // HEAD_DIM
    blocks = rows // BLOCK
    slab = lax.axis_index("seq")
    slabs = lax.axis_size("seq")
    has_before = slab > 0
    has_after = slab < slabs - 1
    score_scale = HEAD_DIM ** (-0.5)
    before_id = {"seq": jnp.maximum(slab - 1, 0)}
    after_id = {"seq": jnp.minimum(slab + 1, slabs - 1)}

    barrier = pltpu.get_barrier_semaphore()

    @pl.when(has_before)
    def _():
        pl.semaphore_signal(barrier, 1, device_id=before_id, device_id_type=MESH)

    @pl.when(has_after)
    def _():
        pl.semaphore_signal(barrier, 1, device_id=after_id, device_id_type=MESH)

    peers = has_before.astype(jnp.int32) + has_after.astype(jnp.int32)
    pl.semaphore_wait(barrier, peers)

    last_rows = pl.ds(rows - BLOCK, BLOCK)
    halo_copies = [
        pltpu.make_async_remote_copy(
            src_ref=ref.at[last_rows],
            dst_ref=halo.at[i],
            send_sem=halo_send.at[i],
            recv_sem=halo_recv.at[i],
            device_id=after_id,
            device_id_type=MESH,
        )
        for i, ref in enumerate((key_ref, value_ref))
    ]
    after_copies = [
        pltpu.make_async_remote_copy(
            src_ref=terms.at[i],
            dst_ref=after.at[i],
            send_sem=after_send.at[i],
            recv_sem=after_recv.at[i],
            device_id=before_id,
            device_id_type=MESH,
        )
        for i in range(2)
    ]

    @pl.when(has_after)
    def _():
        for copy in halo_copies:
            copy.start()

    row_pos = lax.broadcasted_iota(jnp.int32, (BLOCK, 2 * BLOCK), 0)
    key_pos = lax.broadcasted_iota(jnp.int32, (BLOCK, 2 * BLOCK), 1)
    in_window = (key_pos > row_pos) & (key_pos <= row_pos + BLOCK)
    in_first = in_window & (slab * rows - BLOCK + key_pos >= 0)

    def block_step(block, allowed, h):
        col = pl.ds(pl.multiple_of(h * HEAD_DIM, HEAD_DIM), HEAD_DIM)
        own = pl.ds(block * BLOCK, BLOCK)
        prev = pl.ds((block - 1) * BLOCK, BLOCK)
        if block == 0:
            before_keys, before_values = halo[0, :, col], halo[1, :, col]
        else:
            before_keys, before_values = key_ref[prev, col], value_ref[prev, col]
        keyset = jnp.concatenate([before_keys, key_ref[own, col]], 0)
        valueset = jnp.concatenate([before_values, value_ref[own, col]], 0)
        queries, upstream = query_ref[own, col], grad_ref[own, col]
        scores = jnp.where(allowed, dot_nt(queries, keyset) * score_scale, NEG_FILL)
        peak = jnp.max(scores, axis=-1, keepdims=True)
        log_total = peak + jnp.log(jnp.sum(jnp.exp(scores - peak), axis=-1, keepdims=True))
        weights = jnp.exp(scores - log_total)
        rounded_weights = weights.astype(jnp.bfloat16)
        attended = dot_nn(rounded_weights, valueset).astype(jnp.bfloat16)
        row_dots = lane_dot(upstream.astype(jnp.float32), attended.astype(jnp.float32))
        weight_grads = dot_nt(upstream, valueset)
        score_grads = (weights * (weight_grads - row_dots)).astype(jnp.bfloat16)
        out_ref[own, col] = attended
        dq_ref[own, col] = (dot_nn(score_grads, keyset) * score_scale).astype(jnp.bfloat16)
        key_terms = dot_tn(score_grads, queries) * score_scale
        value_terms = dot_tn(rounded_weights, upstream)
        for i, sums in enumerate((key_terms, value_terms)):
            dst = (dk_ref, dv_ref)[i]
            if block == blocks - 1:
                held[i, block, :, col] = sums[BLOCK:]
            else:
                total = sums[BLOCK:] + held[i, block, :, col]
                dst[own, col] = total.astype(jnp.bfloat16)
            if block > 0:
                held[i, block - 1, :, col] = sums[:BLOCK]
            else:
                terms[i, :, col] = sums[:BLOCK].astype(jnp.bfloat16)

    for block in range(blocks - 1, 0, -1):

        def body(h, carry, block=block):
            block_step(block, in_window, h)
            return carry

        lax.fori_loop(0, heads, body, 0)

    @pl.when(has_before)
    def _():
        for copy in halo_copies:
            copy.wait_recv()

    @pl.when(jnp.logical_not(has_before))
    def _():
        halo[...] = jnp.zeros_like(halo)

    def first_body(h, carry):
        block_step(0, in_first, h)
        return carry

    lax.fori_loop(0, heads, first_body, 0)

    @pl.when(has_before)
    def _():
        for copy in after_copies:
            copy.start()

    @pl.when(has_after)
    def _():
        for copy in after_copies:
            copy.wait_recv()

    @pl.when(jnp.logical_not(has_after))
    def _():
        after[...] = jnp.zeros_like(after)

    for i, dst in enumerate((dk_ref, dv_ref)):
        dst[last_rows, :] = (held[i, blocks - 1] + after[i].astype(jnp.float32)).astype(
            jnp.bfloat16
        )

    @pl.when(has_before)
    def _():
        for copy in after_copies:
            copy.wait_send()

    @pl.when(has_after)
    def _():
        for copy in halo_copies:
            copy.wait_send()


def fused_kernel(span, hop, *refs):
    ins, outs = refs[:4], refs[4:8]
    gathered, results, halo, held, terms, after = refs[8:14]
    sems = refs[14:]
    is_band = lax.axis_index("head") < lax.axis_size("head") // 2

    @pl.when(is_band)
    def _():
        band_role(ins, outs, halo, held, terms, after, sems[5:])

    @pl.when(jnp.logical_not(is_band))
    def _():
        strided_role(span, hop, ins, outs, gathered, results, sems[:5])


def place_kernel(*refs):
    made, outs, held, in_sem, out_sem = refs[:4], refs[4:8], refs[8], refs[9], refs[10]
    takes = [pltpu.make_async_copy(made[i], held.at[i], in_sem.at[i]) for i in range(4)]
    gives = [pltpu.make_async_copy(held.at[i], outs[i], out_sem.at[i]) for i in range(4)]
    for copy in takes:
        copy.start()
    for take, give in zip(takes, gives):
        take.wait()
        give.start()
    for copy in gives:
        copy.wait()


def placed(made):
    anywhere = pl.BlockSpec(memory_space=pl.ANY)
    shape, dtype = made[0].shape, made[0].dtype
    return tuple(
        pl.pallas_call(
            place_kernel,
            out_shape=[jax.ShapeDtypeStruct(shape, dtype)] * 4,
            in_specs=[anywhere] * 4,
            out_specs=[anywhere] * 4,
            scratch_shapes=[
                pltpu.VMEM((4, *shape), dtype),
                pltpu.SemaphoreType.DMA((4,)),
                pltpu.SemaphoreType.DMA((4,)),
            ],
        )(*made)
    )


def fused_shards(span, hop, *tensors):
    rows, width = tensors[0].shape
    piece = rows // span
    chunks = width // (CHUNK_HEADS * HEAD_DIM)
    copy_sems = pltpu.SemaphoreType.DMA((chunks, span - 1, 4))
    pair_sems = pltpu.SemaphoreType.DMA((2,))
    vmem = pl.BlockSpec(memory_space=pltpu.VMEM)
    return placed(
        pl.pallas_call(
            functools.partial(fused_kernel, span, hop),
            out_shape=[jax.ShapeDtypeStruct((rows, width), jnp.bfloat16)] * 4,
            in_specs=[vmem] * 4,
            out_specs=[vmem] * 4,
            scratch_shapes=[
                pltpu.VMEM((4, span, piece, width), jnp.bfloat16),
                pltpu.VMEM((4, span, piece, width), jnp.bfloat16),
                pltpu.VMEM((2, BLOCK, width), jnp.bfloat16),
                pltpu.VMEM((2, rows // BLOCK, BLOCK, width), jnp.float32),
                pltpu.VMEM((2, BLOCK, width), jnp.bfloat16),
                pltpu.VMEM((2, BLOCK, width), jnp.bfloat16),
                copy_sems,
                copy_sems,
                copy_sems,
                copy_sems,
                pltpu.SemaphoreType.DMA((4,)),
                pair_sems,
                pair_sems,
                pair_sems,
                pair_sems,
            ],
            compiler_params=pltpu.CompilerParams(collective_id=0, has_side_effects=True),
        )(*tensors)
    )


def shards(query_rows, key_rows, value_rows, grad_out):
    rows = query_rows.shape[0]
    hop = STRIDE // rows
    span = lax.axis_size("seq") // hop
    if span <= 8 and rows % (span * ROW_TILE) == 0:
        return fused_shards(span, hop, query_rows, key_rows, value_rows, grad_out)
    return swapped_shards(query_rows, key_rows, value_rows, grad_out)


def solution(mesh):
    return jax.shard_map(
        shards,
        mesh=mesh,
        in_specs=(P("seq", "head"), P("seq", "head"), P("seq", "head"), P("seq", "head")),
        out_specs=(P("seq", "head"), P("seq", "head"), P("seq", "head"), P("seq", "head")),
        check_vma=False,
    )
```

```python
import functools

import jax
import jax.numpy as jnp
from jax import lax
from jax.experimental import pallas as pl
from jax.experimental.pallas import tpu as pltpu
from jax.sharding import PartitionSpec as P

HEAD_DIM = 128
BLOCK = 128
STRIDE = 512


NEG_FILL = -1e30


def swapped(value, axis, stride):
    mask = 2**stride
    pairs = [(source, source ^ mask) for source in range(lax.axis_size(axis))]
    return lax.ppermute(value, axis, pairs)


def passed_along(shard, axis, by):
    size = lax.axis_size(axis)
    pairs = [(i, i + by) for i in range(size) if 0 <= i + by < size]
    return lax.ppermute(shard, axis, pairs)


def attend(queries, keyset, valueset, upstream, allowed, score_scale):
    scores = (
        jnp.einsum("...qd,...kd->...qk", queries, keyset, preferred_element_type=jnp.float32)
        * score_scale
    )
    scores = jnp.where(allowed, scores, NEG_FILL)
    row_peak = jnp.max(scores, axis=-1, keepdims=True)
    log_total = row_peak + jnp.log(jnp.sum(jnp.exp(scores - row_peak), axis=-1, keepdims=True))
    weights = jnp.exp(scores - log_total)
    rounded_weights = weights.astype(jnp.bfloat16)
    attended = jnp.einsum(
        "...qk,...kd->...qd", rounded_weights, valueset, preferred_element_type=jnp.float32
    ).astype(jnp.bfloat16)
    if upstream is None:
        return attended
    out_float = lax.optimization_barrier(attended).astype(jnp.float32)
    row_dots = jnp.sum(upstream.astype(jnp.float32) * out_float, axis=-1, keepdims=True)
    weight_grads = jnp.einsum(
        "...qd,...kd->...qk", upstream, valueset, preferred_element_type=jnp.float32
    )
    score_grads = (weights * (weight_grads - row_dots)).astype(jnp.bfloat16)
    grad_query = (
        jnp.einsum("...qk,...kd->...qd", score_grads, keyset, preferred_element_type=jnp.float32)
        * score_scale
    ).astype(jnp.bfloat16)
    grad_keys = (
        jnp.einsum("...qk,...qd->...kd", score_grads, queries, preferred_element_type=jnp.float32)
        * score_scale
    )
    grad_values = jnp.einsum(
        "...qk,...qd->...kd", rounded_weights, upstream, preferred_element_type=jnp.float32
    )
    return (attended, grad_query, grad_keys, grad_values)


def swapped_shards(query_rows, key_rows, value_rows, grad_out):
    local_rows, full_width = query_rows.shape
    half_heads = full_width // (2 * HEAD_DIM)
    score_scale = HEAD_DIM ** (-0.5)
    head_count = lax.axis_size("head")
    pair_bit = head_count.bit_length() - 2
    band_holder = lax.axis_index("head") < head_count // 2

    def halves(tensor):
        return tensor.reshape(local_rows, 2, half_heads, HEAD_DIM)

    split_in = [halves(tensor) for tensor in (query_rows, key_rows, value_rows, grad_out)]
    outgoing = [jnp.where(band_holder, tensor[:, 1], tensor[:, 0]) for tensor in split_in]
    staying = [jnp.where(band_holder, tensor[:, 0], tensor[:, 1]) for tensor in split_in]
    incoming = swapped((outgoing[0], outgoing[1], outgoing[2], outgoing[3]), "head", pair_bit)
    band_in = [
        jnp.where(band_holder, own_part, other_part)
        for own_part, other_part in zip(staying, incoming)
    ]
    stride_in = [
        jnp.where(band_holder, other_part, own_part)
        for own_part, other_part in zip(staying, incoming)
    ]
    block_count = local_rows // BLOCK
    band_query, band_keys, band_values, band_grads = band_in
    before_rows = passed_along(
        (band_keys[local_rows - BLOCK :], band_values[local_rows - BLOCK :]), "seq", 1
    )

    def blocked(tensor):
        return jnp.swapaxes(tensor.reshape(block_count, BLOCK, half_heads, HEAD_DIM), 1, 2)

    def windowed(earlier, tensor):
        joined = jnp.concatenate([earlier, tensor], 0).reshape(
            block_count + 1, BLOCK, half_heads, HEAD_DIM
        )
        return jnp.swapaxes(jnp.concatenate([joined[:-1], joined[1:]], 1), 1, 2)

    anchor = lax.axis_index("seq") * local_rows
    row_pos = jnp.arange(BLOCK)[:, None]
    key_pos = jnp.arange(2 * BLOCK)[None, :]
    block_pos = jnp.arange(block_count)[:, None, None, None]
    allowed = (
        (key_pos > row_pos)
        & (key_pos <= row_pos + BLOCK)
        & (anchor + (block_pos - 1) * BLOCK + key_pos >= 0)
    )
    band_out, band_dq, key_terms, value_terms = attend(
        blocked(band_query),
        windowed(before_rows[0], band_keys),
        windowed(before_rows[1], band_values),
        blocked(band_grads),
        allowed,
        score_scale,
    )

    def unblocked(tensor):
        return jnp.swapaxes(tensor, 1, 2).reshape(local_rows, half_heads, HEAD_DIM)

    def folded(term_sums):
        spread = jnp.swapaxes(term_sums, 1, 2)
        zero_block = jnp.zeros((1, BLOCK, half_heads, HEAD_DIM), jnp.float32)
        return jnp.concatenate([spread[:, :BLOCK], zero_block], 0) + jnp.concatenate(
            [zero_block, spread[:, BLOCK:]], 0
        )

    key_total = folded(key_terms)
    value_total = folded(value_terms)
    after_terms = (
        passed_along(key_total[0].astype(jnp.bfloat16), "seq", -1).astype(jnp.float32),
        passed_along(value_total[0].astype(jnp.bfloat16), "seq", -1).astype(jnp.float32),
    )
    band_dk = (
        key_total[1:]
        .at[block_count - 1]
        .add(after_terms[0])
        .reshape(local_rows, half_heads, HEAD_DIM)
        .astype(jnp.bfloat16)
    )
    band_dv = (
        value_total[1:]
        .at[block_count - 1]
        .add(after_terms[1])
        .reshape(local_rows, half_heads, HEAD_DIM)
        .astype(jnp.bfloat16)
    )
    band_results = (unblocked(band_out), unblocked(band_dq), band_dk, band_dv)
    seq_count = lax.axis_size("seq")
    group_count = STRIDE // seq_count
    group_span = local_rows // group_count

    def offset_in(tensor):
        return tensor.reshape(local_rows // seq_count, seq_count, half_heads, HEAD_DIM)

    def regroup(tensor):
        return jnp.transpose(
            tensor.reshape(group_span, group_count, tensor.shape[2], HEAD_DIM), (1, 2, 0, 3)
        )

    def restore(tensor):
        return jnp.transpose(tensor, (2, 0, 1, 3)).reshape(local_rows, 1, tensor.shape[1], HEAD_DIM)

    causal_mask = jnp.arange(group_span)[None, :] <= jnp.arange(group_span)[:, None]
    stride_query, stride_keys, stride_values, stride_grads = [
        offset_in(tensor) for tensor in stride_in
    ]
    pieces = (
        lax.all_to_all(stride_query, "seq", split_axis=1, concat_axis=0, tiled=True),
        lax.all_to_all(stride_keys, "seq", split_axis=1, concat_axis=0, tiled=True),
        lax.all_to_all(stride_values, "seq", split_axis=1, concat_axis=0, tiled=True),
    )
    attended = attend(
        regroup(pieces[0]), regroup(pieces[1]), regroup(pieces[2]), None, causal_mask, score_scale
    )
    stride_out = lax.all_to_all(restore(attended), "seq", split_axis=0, concat_axis=1, tiled=True)
    pieces = (
        lax.all_to_all(stride_query, "seq", split_axis=1, concat_axis=0, tiled=True),
        lax.all_to_all(stride_keys, "seq", split_axis=1, concat_axis=0, tiled=True),
        lax.all_to_all(stride_values, "seq", split_axis=1, concat_axis=0, tiled=True),
        lax.all_to_all(stride_grads, "seq", split_axis=1, concat_axis=0, tiled=True),
    )
    results = attend(
        regroup(pieces[0]),
        regroup(pieces[1]),
        regroup(pieces[2]),
        regroup(pieces[3]),
        causal_mask,
        score_scale,
    )
    stride_dq = lax.all_to_all(restore(results[1]), "seq", split_axis=0, concat_axis=1, tiled=True)
    stride_dk = lax.all_to_all(
        restore(results[2].astype(jnp.bfloat16)), "seq", split_axis=0, concat_axis=1, tiled=True
    )
    stride_dv = lax.all_to_all(
        restore(results[3].astype(jnp.bfloat16)), "seq", split_axis=0, concat_axis=1, tiled=True
    )
    stride_results = tuple(
        (
            tensor.reshape(local_rows, half_heads, HEAD_DIM)
            for tensor in (stride_out, stride_dq, stride_dk, stride_dv)
        )
    )
    send_back = [
        jnp.where(band_holder, stride_part, band_part)
        for band_part, stride_part in zip(band_results, stride_results)
    ]
    keep_back = [
        jnp.where(band_holder, band_part, stride_part)
        for band_part, stride_part in zip(band_results, stride_results)
    ]
    returned = swapped((send_back[0], send_back[1], send_back[2], send_back[3]), "head", pair_bit)
    outputs = []
    for kept_part, got_part in zip(keep_back, returned):
        first_half = jnp.where(band_holder, kept_part, got_part)
        second_half = jnp.where(band_holder, got_part, kept_part)
        outputs.append(jnp.stack([first_half, second_half], 1).reshape(local_rows, full_width))
    return (outputs[0], outputs[1], outputs[2], outputs[3])


MESH = pl.DeviceIdType.MESH
CHUNK_HEADS = 2
ROW_TILE = 16


def lane_dot(left, right):
    return jnp.sum(left * right, axis=-1, keepdims=True)


def as_bf16(tensor):
    return tensor.astype(jnp.bfloat16).astype(jnp.float32)


def piece_sizes(rows, span):
    even = rows // span
    shift = even // 4 // ROW_TILE * ROW_TILE if span == 4 else 0
    return [even + shift if t in (0, span - 1) else even - shift for t in range(span)]


def needed(source, span):
    return ((0, 3) if source > 0 else ()) + ((1, 2) if source < span - 1 else ())


def returned_to(target, span):
    return ((0, 1) if target > 0 else ()) + ((2, 3) if target < span - 1 else ())


def softmax_weights(scores):
    peak = functools.reduce(jnp.maximum, scores)
    total = functools.reduce(jnp.add, [jnp.exp(score - peak) for score in scores])
    log_total = peak + jnp.log(total)
    return [jnp.exp(score - log_total) for score in scores]


def strided_tile(span, score_scale, queries, keyset, valueset, upstream, last_score, last_grad):
    last = span - 1
    attended, grad_query = [None] * span, [None] * span
    grad_keys, grad_values = [None] * span, [None] * span

    def plus(total, term):
        return term if total is None else total + term

    for p in range(1, span):
        count = min(p + 1, last)
        scores = [lane_dot(queries[p], keyset[j]) * score_scale for j in range(count)]
        grads = [lane_dot(upstream[p], valueset[j]) for j in range(count)]
        if p == last:
            scores.append(last_score)
            grads.append(last_grad)
        weights = softmax_weights(scores)
        rounded_weights = [as_bf16(weight) for weight in weights]
        out, dq = None, None
        for j in range(count):
            out = plus(out, rounded_weights[j] * valueset[j])
            grad_values[j] = plus(grad_values[j], rounded_weights[j] * upstream[p])
        attended[p] = out.astype(jnp.bfloat16)
        if p == last:
            row_dots = functools.reduce(
                jnp.add, [weight * grad for weight, grad in zip(rounded_weights, grads)]
            )
        else:
            row_dots = lane_dot(upstream[p], attended[p].astype(jnp.float32))
        for j in range(count):
            score_grads = as_bf16(weights[j] * (grads[j] - row_dots))
            dq = plus(dq, score_grads * keyset[j])
            grad_keys[j] = plus(grad_keys[j], score_grads * queries[p])
        grad_query[p] = dq * score_scale
    last_weight = rounded_weights[last]
    last_score_grad = as_bf16(weights[last] * (grads[last] - row_dots))
    grad_keys = [tensor if tensor is None else tensor * score_scale for tensor in grad_keys]
    return (attended, grad_query, grad_keys, grad_values), last_weight, last_score_grad


def strided_role(place, span, hop, ins, outs, buffers, sems):
    gathered, results, pair_in, pair_use, pair_out, pair_back = buffers
    in_send, in_recv, out_send, out_recv, own_sem, ps_send, ps_recv, pb_send, pb_recv = sems
    rows, width = ins[0].shape
    sizes = piece_sizes(rows, span)
    starts = [sum(sizes[:t]) for t in range(span)]
    last = span - 1
    size = sizes[place]
    offset = lax.rem(lax.axis_index("seq"), hop)
    chunk_cols = CHUNK_HEADS * HEAD_DIM
    chunks = width // chunk_cols
    heads = width // HEAD_DIM
    score_scale = HEAD_DIM ** (-0.5)
    others = [(place + step) % span for step in range(1, span)]
    mine = pl.ds(starts[place], size)

    def seq_of(member):
        return {"seq": member * hop + offset}

    def rows_of(member):
        return pl.ds(starts[member], sizes[member])

    def remote(src, dst, send, recv, member):
        return pltpu.make_async_remote_copy(
            src_ref=src,
            dst_ref=dst,
            send_sem=send,
            recv_sem=recv,
            device_id=seq_of(member),
            device_id_type=MESH,
        )

    barrier = pltpu.get_barrier_semaphore()
    for member in others:
        pl.semaphore_signal(barrier, 1, device_id=seq_of(member), device_id_type=MESH)
    pl.semaphore_wait(barrier, span - 1)

    own = []
    for i in range(4):
        own.append(
            pltpu.make_async_copy(
                ins[i].at[mine], gathered.at[i, place, pl.ds(0, size)], own_sem.at[i]
            )
        )
        own[-1].start()
    sent = []

    def send_chunk(c):
        cols = pl.ds(c * chunk_cols, chunk_cols)
        for member in others:
            for i in needed(place, span):
                copy = remote(
                    ins[i].at[rows_of(member), cols],
                    gathered.at[i, place, pl.ds(0, sizes[member]), cols],
                    in_send.at[c, member, i],
                    in_recv.at[c, place, i],
                    member,
                )
                copy.start()
                sent.append(copy)

    send_chunk(0)
    lanes = lax.broadcasted_iota(jnp.int32, (ROW_TILE, 128), 1)
    if place == last:

        def pair_body(index, carry):
            row = pl.ds(pl.multiple_of(index * ROW_TILE, ROW_TILE), ROW_TILE)
            kept = jnp.zeros((ROW_TILE, 128), jnp.float32)
            for h in range(heads):
                col = pl.ds(h * HEAD_DIM, HEAD_DIM)
                q, k, v, g = [ref[row, col].astype(jnp.float32) for ref in ins]
                kept = jnp.where(lanes == 2 * h, lane_dot(q, k) * score_scale, kept)
                kept = jnp.where(lanes == 2 * h + 1, lane_dot(g, v), kept)
            pair_in[row, :] = kept
            return carry

        lax.fori_loop(0, rows // ROW_TILE, pair_body, 0)
        for member in others:
            copy = remote(
                pair_in.at[rows_of(member)],
                pair_use.at[pl.ds(0, sizes[member])],
                ps_send.at[member],
                ps_recv.at[0],
                member,
            )
            copy.start()
            sent.append(copy)
        pair_use[pl.ds(0, size), :] = pair_in[mine, :]
    for c in range(1, chunks):
        send_chunk(c)
    for copy in own:
        copy.wait()
    if place != last:
        piece = pair_use.at[pl.ds(0, size)]
        remote(piece, piece, ps_send.at[last], ps_recv.at[0], last).wait_recv()
    tiles = size // ROW_TILE
    for c in range(chunks):
        cols = pl.ds(c * chunk_cols, chunk_cols)
        for member in others:
            for i in needed(member, span):
                piece = gathered.at[i, member, pl.ds(0, size), cols]
                remote(
                    piece, piece, in_send.at[c, member, i], in_recv.at[c, member, i], member
                ).wait_recv()
        pair_out[c] = jnp.zeros(pair_out.shape[1:], jnp.float32)

        def body(index, carry, c=c):
            row = pl.ds(pl.multiple_of(lax.rem(index, tiles) * ROW_TILE, ROW_TILE), ROW_TILE)
            head = index // tiles
            col = pl.ds(pl.multiple_of(c * chunk_cols + head * HEAD_DIM, HEAD_DIM), HEAD_DIM)
            loaded = [
                [
                    gathered[i, j, row, col].astype(jnp.float32) if i in needed(j, span) else None
                    for j in range(span)
                ]
                for i in range(4)
            ]
            pairs = pair_use[row, :]
            lane = 2 * (c * CHUNK_HEADS + head)

            def at_lane(k):
                return jnp.sum(jnp.where(lanes == k, pairs, 0.0), axis=-1, keepdims=True)

            made, weight, grad = strided_tile(
                span, score_scale, *loaded, at_lane(lane), at_lane(lane + 1)
            )
            for j in range(span):
                for i in returned_to(j, span):
                    results[i, j, row, col] = made[i][j].astype(jnp.bfloat16)
            kept = pair_out[c, row, :]
            kept = jnp.where(lanes == 2 * head, weight, kept)
            pair_out[c, row, :] = jnp.where(lanes == 2 * head + 1, grad, kept)
            return carry

        lax.fori_loop(0, tiles * CHUNK_HEADS, body, 0)
        for member in others:
            for i in returned_to(member, span):
                copy = remote(
                    results.at[i, member, pl.ds(0, size), cols],
                    outs[i].at[mine, cols],
                    out_send.at[c, member, i],
                    out_recv.at[c, place, i],
                    member,
                )
                copy.start()
                sent.append(copy)
        if place != last:
            copy = remote(
                pair_out.at[c, pl.ds(0, size)],
                pair_back.at[c, mine],
                pb_send.at[c],
                pb_recv.at[c, place],
                last,
            )
            copy.start()
            sent.append(copy)
        else:
            pair_back[c, mine, :] = pair_out[c, pl.ds(0, size), :]
    for i in returned_to(place, span):
        outs[i][mine, :] = results[i, place, pl.ds(0, size), :]
    big = rows // 4
    big_lanes = lax.broadcasted_iota(jnp.int32, (big, 128), 1)
    for c in range(chunks):
        cols = pl.ds(c * chunk_cols, chunk_cols)
        for member in others:
            for i in returned_to(place, span):
                piece = outs[i].at[rows_of(member), cols]
                remote(
                    piece, piece, out_send.at[c, member, i], out_recv.at[c, member, i], member
                ).wait_recv()
            if place == last:
                piece = pair_back.at[c, rows_of(member)]
                remote(piece, piece, pb_send.at[c], pb_recv.at[c, member], member).wait_recv()
        if place not in (0, last):
            continue

        def close(index, carry, c=c):
            row = pl.ds(pl.multiple_of(lax.rem(index, 4) * big, big), big)
            head = index // 4
            col = pl.ds(pl.multiple_of(c * chunk_cols + head * HEAD_DIM, HEAD_DIM), HEAD_DIM)
            q, k, v, g = [ref[row, col].astype(jnp.float32) for ref in ins]
            if place == last:
                kept = pair_back[c, row, :]
                weight, grad = [
                    jnp.sum(jnp.where(big_lanes == 2 * head + n, kept, 0.0), -1, keepdims=True)
                    for n in range(2)
                ]
                terms = (weight * v, grad * k * score_scale, grad * q * score_scale, weight * g)
            else:
                (weight,) = softmax_weights([lane_dot(q, k) * score_scale])
                out = as_bf16(weight) * v
                row_dots = lane_dot(g, as_bf16(out))
                grad = as_bf16(weight * (lane_dot(g, v) - row_dots))
                terms = (out, grad * k * score_scale, grad * q * score_scale, as_bf16(weight) * g)
            for i in range(4):
                total = terms[i]
                if i in returned_to(place, span):
                    total = total + outs[i][row, col].astype(jnp.float32)
                outs[i][row, col] = total.astype(jnp.bfloat16)
            return carry

        lax.fori_loop(0, 4 * CHUNK_HEADS, close, 0)
    for copy in sent:
        copy.wait_send()


def dot_nt(left, right):
    return lax.dot_general(left, right, (((1,), (1,)), ((), ())), preferred_element_type=jnp.float32)


def dot_nn(left, right):
    return lax.dot_general(left, right, (((1,), (0,)), ((), ())), preferred_element_type=jnp.float32)


def dot_tn(left, right):
    return lax.dot_general(left, right, (((0,), (0,)), ((), ())), preferred_element_type=jnp.float32)


def band_role(ins, outs, halo, held, terms, after, sems):
    halo_send, halo_recv, after_send, after_recv = sems
    query_ref, key_ref, value_ref, grad_ref = ins
    out_ref, dq_ref, dk_ref, dv_ref = outs
    rows, width = query_ref.shape
    heads = width // HEAD_DIM
    blocks = rows // BLOCK
    slab = lax.axis_index("seq")
    slabs = lax.axis_size("seq")
    has_before = slab > 0
    has_after = slab < slabs - 1
    score_scale = HEAD_DIM ** (-0.5)
    before_id = {"seq": jnp.maximum(slab - 1, 0)}
    after_id = {"seq": jnp.minimum(slab + 1, slabs - 1)}

    barrier = pltpu.get_barrier_semaphore()

    @pl.when(has_before)
    def _():
        pl.semaphore_signal(barrier, 1, device_id=before_id, device_id_type=MESH)

    @pl.when(has_after)
    def _():
        pl.semaphore_signal(barrier, 1, device_id=after_id, device_id_type=MESH)

    peers = has_before.astype(jnp.int32) + has_after.astype(jnp.int32)
    pl.semaphore_wait(barrier, peers)

    last_rows = pl.ds(rows - BLOCK, BLOCK)
    halo_copies = [
        pltpu.make_async_remote_copy(
            src_ref=ref.at[last_rows],
            dst_ref=halo.at[i],
            send_sem=halo_send.at[i],
            recv_sem=halo_recv.at[i],
            device_id=after_id,
            device_id_type=MESH,
        )
        for i, ref in enumerate((key_ref, value_ref))
    ]
    after_copies = [
        pltpu.make_async_remote_copy(
            src_ref=terms.at[i],
            dst_ref=after.at[i],
            send_sem=after_send.at[i],
            recv_sem=after_recv.at[i],
            device_id=before_id,
            device_id_type=MESH,
        )
        for i in range(2)
    ]

    @pl.when(has_after)
    def _():
        for copy in halo_copies:
            copy.start()

    row_pos = lax.broadcasted_iota(jnp.int32, (BLOCK, 2 * BLOCK), 0)
    key_pos = lax.broadcasted_iota(jnp.int32, (BLOCK, 2 * BLOCK), 1)
    in_window = (key_pos > row_pos) & (key_pos <= row_pos + BLOCK)
    in_first = in_window & (slab * rows - BLOCK + key_pos >= 0)

    def block_step(block, allowed, h):
        col = pl.ds(pl.multiple_of(h * HEAD_DIM, HEAD_DIM), HEAD_DIM)
        own = pl.ds(block * BLOCK, BLOCK)
        prev = pl.ds((block - 1) * BLOCK, BLOCK)
        if block == 0:
            before_keys, before_values = halo[0, :, col], halo[1, :, col]
        else:
            before_keys, before_values = key_ref[prev, col], value_ref[prev, col]
        keyset = jnp.concatenate([before_keys, key_ref[own, col]], 0)
        valueset = jnp.concatenate([before_values, value_ref[own, col]], 0)
        queries, upstream = query_ref[own, col], grad_ref[own, col]
        scores = jnp.where(allowed, dot_nt(queries, keyset) * score_scale, NEG_FILL)
        peak = jnp.max(scores, axis=-1, keepdims=True)
        log_total = peak + jnp.log(jnp.sum(jnp.exp(scores - peak), axis=-1, keepdims=True))
        weights = jnp.exp(scores - log_total)
        rounded_weights = weights.astype(jnp.bfloat16)
        attended = dot_nn(rounded_weights, valueset).astype(jnp.bfloat16)
        row_dots = lane_dot(upstream.astype(jnp.float32), attended.astype(jnp.float32))
        weight_grads = dot_nt(upstream, valueset)
        score_grads = (weights * (weight_grads - row_dots)).astype(jnp.bfloat16)
        out_ref[own, col] = attended
        dq_ref[own, col] = (dot_nn(score_grads, keyset) * score_scale).astype(jnp.bfloat16)
        key_terms = dot_tn(score_grads, queries) * score_scale
        value_terms = dot_tn(rounded_weights, upstream)
        for i, sums in enumerate((key_terms, value_terms)):
            dst = (dk_ref, dv_ref)[i]
            if block == blocks - 1:
                held[i, block, :, col] = sums[BLOCK:]
            else:
                total = sums[BLOCK:] + held[i, block, :, col]
                dst[own, col] = total.astype(jnp.bfloat16)
            if block > 0:
                held[i, block - 1, :, col] = sums[:BLOCK]
            else:
                terms[i, :, col] = sums[:BLOCK].astype(jnp.bfloat16)

    for block in range(blocks - 1, 0, -1):

        def body(h, carry, block=block):
            block_step(block, in_window, h)
            return carry

        lax.fori_loop(0, heads, body, 0)

    @pl.when(has_before)
    def _():
        for copy in halo_copies:
            copy.wait_recv()

    @pl.when(jnp.logical_not(has_before))
    def _():
        halo[...] = jnp.zeros_like(halo)

    def first_body(h, carry):
        block_step(0, in_first, h)
        return carry

    lax.fori_loop(0, heads, first_body, 0)

    @pl.when(has_before)
    def _():
        for copy in after_copies:
            copy.start()

    @pl.when(has_after)
    def _():
        for copy in after_copies:
            copy.wait_recv()

    @pl.when(jnp.logical_not(has_after))
    def _():
        after[...] = jnp.zeros_like(after)

    for i, dst in enumerate((dk_ref, dv_ref)):
        dst[last_rows, :] = (held[i, blocks - 1] + after[i].astype(jnp.float32)).astype(
            jnp.bfloat16
        )

    @pl.when(has_before)
    def _():
        for copy in after_copies:
            copy.wait_send()

    @pl.when(has_after)
    def _():
        for copy in halo_copies:
            copy.wait_send()


def fused_kernel(span, hop, *refs):
    ins, outs = refs[:4], refs[4:8]
    buffers, (halo, held, terms, after) = refs[8:14], refs[14:18]
    sems = refs[18:]
    is_band = lax.axis_index("head") < lax.axis_size("head") // 2
    place = lax.axis_index("seq") // hop

    @pl.when(is_band)
    def _():
        band_role(ins, outs, halo, held, terms, after, sems[9:])

    for t in range(span):

        @pl.when(jnp.logical_not(is_band) & (place == t))
        def _(t=t):
            strided_role(t, span, hop, ins, outs, buffers, sems[:9])


def place_kernel(*refs):
    made, outs, held, in_sem, out_sem = refs[:4], refs[4:8], refs[8], refs[9], refs[10]
    takes = [pltpu.make_async_copy(made[i], held.at[i], in_sem.at[i]) for i in range(4)]
    gives = [pltpu.make_async_copy(held.at[i], outs[i], out_sem.at[i]) for i in range(4)]
    for copy in takes:
        copy.start()
    for take, give in zip(takes, gives):
        take.wait()
        give.start()
    for copy in gives:
        copy.wait()


def placed(made):
    anywhere = pl.BlockSpec(memory_space=pl.ANY)
    shape, dtype = made[0].shape, made[0].dtype
    return tuple(
        pl.pallas_call(
            place_kernel,
            out_shape=[jax.ShapeDtypeStruct(shape, dtype)] * 4,
            in_specs=[anywhere] * 4,
            out_specs=[anywhere] * 4,
            scratch_shapes=[
                pltpu.VMEM((4, *shape), dtype),
                pltpu.SemaphoreType.DMA((4,)),
                pltpu.SemaphoreType.DMA((4,)),
            ],
        )(*made)
    )


def fused_shards(span, hop, *tensors):
    rows, width = tensors[0].shape
    piece = max(piece_sizes(rows, span))
    chunks = width // (CHUNK_HEADS * HEAD_DIM)
    copy_sems = pltpu.SemaphoreType.DMA((chunks, span, 4))
    pair_sems = pltpu.SemaphoreType.DMA((2,))
    vmem = pl.BlockSpec(memory_space=pltpu.VMEM)
    return placed(
        pl.pallas_call(
            functools.partial(fused_kernel, span, hop),
            out_shape=[jax.ShapeDtypeStruct((rows, width), jnp.bfloat16)] * 4,
            in_specs=[vmem] * 4,
            out_specs=[vmem] * 4,
            scratch_shapes=[
                pltpu.VMEM((4, span, piece, width), jnp.bfloat16),
                pltpu.VMEM((4, span, piece, width), jnp.bfloat16),
                pltpu.VMEM((rows, 128), jnp.float32),
                pltpu.VMEM((piece, 128), jnp.float32),
                pltpu.VMEM((chunks, piece, 128), jnp.float32),
                pltpu.VMEM((chunks, rows, 128), jnp.float32),
                pltpu.VMEM((2, BLOCK, width), jnp.bfloat16),
                pltpu.VMEM((2, rows // BLOCK, BLOCK, width), jnp.float32),
                pltpu.VMEM((2, BLOCK, width), jnp.bfloat16),
                pltpu.VMEM((2, BLOCK, width), jnp.bfloat16),
                copy_sems,
                copy_sems,
                copy_sems,
                copy_sems,
                pltpu.SemaphoreType.DMA((4,)),
                pltpu.SemaphoreType.DMA((span,)),
                pltpu.SemaphoreType.DMA((1,)),
                pltpu.SemaphoreType.DMA((chunks,)),
                pltpu.SemaphoreType.DMA((chunks, span)),
                pair_sems,
                pair_sems,
                pair_sems,
                pair_sems,
            ],
            compiler_params=pltpu.CompilerParams(collective_id=0, has_side_effects=True),
        )(*tensors)
    )


def shards(query_rows, key_rows, value_rows, grad_out):
    rows = query_rows.shape[0]
    hop = STRIDE // rows
    span = lax.axis_size("seq") // hop
    if 2 <= span <= 8 and rows % (span * ROW_TILE) == 0:
        return fused_shards(span, hop, query_rows, key_rows, value_rows, grad_out)
    return swapped_shards(query_rows, key_rows, value_rows, grad_out)


def solution(mesh):
    return jax.shard_map(
        shards,
        mesh=mesh,
        in_specs=(P("seq", "head"), P("seq", "head"), P("seq", "head"), P("seq", "head")),
        out_specs=(P("seq", "head"), P("seq", "head"), P("seq", "head"), P("seq", "head")),
        check_vma=False,
    )
```

```python
import functools

import jax
import jax.numpy as jnp
from jax import lax
from jax.experimental import pallas as pl
from jax.experimental.pallas import tpu as pltpu
from jax.sharding import PartitionSpec as P

HEAD_DIM = 128
BLOCK = 128
STRIDE = 512


NEG_FILL = -1e30


def swapped(value, axis, stride):
    mask = 2**stride
    pairs = [(source, source ^ mask) for source in range(lax.axis_size(axis))]
    return lax.ppermute(value, axis, pairs)


def passed_along(shard, axis, by):
    size = lax.axis_size(axis)
    pairs = [(i, i + by) for i in range(size) if 0 <= i + by < size]
    return lax.ppermute(shard, axis, pairs)


def attend(queries, keyset, valueset, upstream, allowed, score_scale):
    scores = (
        jnp.einsum("...qd,...kd->...qk", queries, keyset, preferred_element_type=jnp.float32)
        * score_scale
    )
    scores = jnp.where(allowed, scores, NEG_FILL)
    row_peak = jnp.max(scores, axis=-1, keepdims=True)
    log_total = row_peak + jnp.log(jnp.sum(jnp.exp(scores - row_peak), axis=-1, keepdims=True))
    weights = jnp.exp(scores - log_total)
    rounded_weights = weights.astype(jnp.bfloat16)
    attended = jnp.einsum(
        "...qk,...kd->...qd", rounded_weights, valueset, preferred_element_type=jnp.float32
    ).astype(jnp.bfloat16)
    if upstream is None:
        return attended
    out_float = lax.optimization_barrier(attended).astype(jnp.float32)
    row_dots = jnp.sum(upstream.astype(jnp.float32) * out_float, axis=-1, keepdims=True)
    weight_grads = jnp.einsum(
        "...qd,...kd->...qk", upstream, valueset, preferred_element_type=jnp.float32
    )
    score_grads = (weights * (weight_grads - row_dots)).astype(jnp.bfloat16)
    grad_query = (
        jnp.einsum("...qk,...kd->...qd", score_grads, keyset, preferred_element_type=jnp.float32)
        * score_scale
    ).astype(jnp.bfloat16)
    grad_keys = (
        jnp.einsum("...qk,...qd->...kd", score_grads, queries, preferred_element_type=jnp.float32)
        * score_scale
    )
    grad_values = jnp.einsum(
        "...qk,...qd->...kd", rounded_weights, upstream, preferred_element_type=jnp.float32
    )
    return (attended, grad_query, grad_keys, grad_values)


def swapped_shards(query_rows, key_rows, value_rows, grad_out):
    local_rows, full_width = query_rows.shape
    half_heads = full_width // (2 * HEAD_DIM)
    score_scale = HEAD_DIM ** (-0.5)
    head_count = lax.axis_size("head")
    pair_bit = head_count.bit_length() - 2
    band_holder = lax.axis_index("head") < head_count // 2

    def halves(tensor):
        return tensor.reshape(local_rows, 2, half_heads, HEAD_DIM)

    split_in = [halves(tensor) for tensor in (query_rows, key_rows, value_rows, grad_out)]
    outgoing = [jnp.where(band_holder, tensor[:, 1], tensor[:, 0]) for tensor in split_in]
    staying = [jnp.where(band_holder, tensor[:, 0], tensor[:, 1]) for tensor in split_in]
    incoming = swapped((outgoing[0], outgoing[1], outgoing[2], outgoing[3]), "head", pair_bit)
    band_in = [
        jnp.where(band_holder, own_part, other_part)
        for own_part, other_part in zip(staying, incoming)
    ]
    stride_in = [
        jnp.where(band_holder, other_part, own_part)
        for own_part, other_part in zip(staying, incoming)
    ]
    block_count = local_rows // BLOCK
    band_query, band_keys, band_values, band_grads = band_in
    before_rows = passed_along(
        (band_keys[local_rows - BLOCK :], band_values[local_rows - BLOCK :]), "seq", 1
    )

    def blocked(tensor):
        return jnp.swapaxes(tensor.reshape(block_count, BLOCK, half_heads, HEAD_DIM), 1, 2)

    def windowed(earlier, tensor):
        joined = jnp.concatenate([earlier, tensor], 0).reshape(
            block_count + 1, BLOCK, half_heads, HEAD_DIM
        )
        return jnp.swapaxes(jnp.concatenate([joined[:-1], joined[1:]], 1), 1, 2)

    anchor = lax.axis_index("seq") * local_rows
    row_pos = jnp.arange(BLOCK)[:, None]
    key_pos = jnp.arange(2 * BLOCK)[None, :]
    block_pos = jnp.arange(block_count)[:, None, None, None]
    allowed = (
        (key_pos > row_pos)
        & (key_pos <= row_pos + BLOCK)
        & (anchor + (block_pos - 1) * BLOCK + key_pos >= 0)
    )
    band_out, band_dq, key_terms, value_terms = attend(
        blocked(band_query),
        windowed(before_rows[0], band_keys),
        windowed(before_rows[1], band_values),
        blocked(band_grads),
        allowed,
        score_scale,
    )

    def unblocked(tensor):
        return jnp.swapaxes(tensor, 1, 2).reshape(local_rows, half_heads, HEAD_DIM)

    def folded(term_sums):
        spread = jnp.swapaxes(term_sums, 1, 2)
        zero_block = jnp.zeros((1, BLOCK, half_heads, HEAD_DIM), jnp.float32)
        return jnp.concatenate([spread[:, :BLOCK], zero_block], 0) + jnp.concatenate(
            [zero_block, spread[:, BLOCK:]], 0
        )

    key_total = folded(key_terms)
    value_total = folded(value_terms)
    after_terms = (
        passed_along(key_total[0].astype(jnp.bfloat16), "seq", -1).astype(jnp.float32),
        passed_along(value_total[0].astype(jnp.bfloat16), "seq", -1).astype(jnp.float32),
    )
    band_dk = (
        key_total[1:]
        .at[block_count - 1]
        .add(after_terms[0])
        .reshape(local_rows, half_heads, HEAD_DIM)
        .astype(jnp.bfloat16)
    )
    band_dv = (
        value_total[1:]
        .at[block_count - 1]
        .add(after_terms[1])
        .reshape(local_rows, half_heads, HEAD_DIM)
        .astype(jnp.bfloat16)
    )
    band_results = (unblocked(band_out), unblocked(band_dq), band_dk, band_dv)
    seq_count = lax.axis_size("seq")
    group_count = STRIDE // seq_count
    group_span = local_rows // group_count

    def offset_in(tensor):
        return tensor.reshape(local_rows // seq_count, seq_count, half_heads, HEAD_DIM)

    def regroup(tensor):
        return jnp.transpose(
            tensor.reshape(group_span, group_count, tensor.shape[2], HEAD_DIM), (1, 2, 0, 3)
        )

    def restore(tensor):
        return jnp.transpose(tensor, (2, 0, 1, 3)).reshape(local_rows, 1, tensor.shape[1], HEAD_DIM)

    causal_mask = jnp.arange(group_span)[None, :] <= jnp.arange(group_span)[:, None]
    stride_query, stride_keys, stride_values, stride_grads = [
        offset_in(tensor) for tensor in stride_in
    ]
    pieces = (
        lax.all_to_all(stride_query, "seq", split_axis=1, concat_axis=0, tiled=True),
        lax.all_to_all(stride_keys, "seq", split_axis=1, concat_axis=0, tiled=True),
        lax.all_to_all(stride_values, "seq", split_axis=1, concat_axis=0, tiled=True),
    )
    attended = attend(
        regroup(pieces[0]), regroup(pieces[1]), regroup(pieces[2]), None, causal_mask, score_scale
    )
    stride_out = lax.all_to_all(restore(attended), "seq", split_axis=0, concat_axis=1, tiled=True)
    pieces = (
        lax.all_to_all(stride_query, "seq", split_axis=1, concat_axis=0, tiled=True),
        lax.all_to_all(stride_keys, "seq", split_axis=1, concat_axis=0, tiled=True),
        lax.all_to_all(stride_values, "seq", split_axis=1, concat_axis=0, tiled=True),
        lax.all_to_all(stride_grads, "seq", split_axis=1, concat_axis=0, tiled=True),
    )
    results = attend(
        regroup(pieces[0]),
        regroup(pieces[1]),
        regroup(pieces[2]),
        regroup(pieces[3]),
        causal_mask,
        score_scale,
    )
    stride_dq = lax.all_to_all(restore(results[1]), "seq", split_axis=0, concat_axis=1, tiled=True)
    stride_dk = lax.all_to_all(
        restore(results[2].astype(jnp.bfloat16)), "seq", split_axis=0, concat_axis=1, tiled=True
    )
    stride_dv = lax.all_to_all(
        restore(results[3].astype(jnp.bfloat16)), "seq", split_axis=0, concat_axis=1, tiled=True
    )
    stride_results = tuple(
        (
            tensor.reshape(local_rows, half_heads, HEAD_DIM)
            for tensor in (stride_out, stride_dq, stride_dk, stride_dv)
        )
    )
    send_back = [
        jnp.where(band_holder, stride_part, band_part)
        for band_part, stride_part in zip(band_results, stride_results)
    ]
    keep_back = [
        jnp.where(band_holder, band_part, stride_part)
        for band_part, stride_part in zip(band_results, stride_results)
    ]
    returned = swapped((send_back[0], send_back[1], send_back[2], send_back[3]), "head", pair_bit)
    outputs = []
    for kept_part, got_part in zip(keep_back, returned):
        first_half = jnp.where(band_holder, kept_part, got_part)
        second_half = jnp.where(band_holder, got_part, kept_part)
        outputs.append(jnp.stack([first_half, second_half], 1).reshape(local_rows, full_width))
    return (outputs[0], outputs[1], outputs[2], outputs[3])


MESH = pl.DeviceIdType.MESH
CHUNK_HEADS = 2
ROW_TILE = 16


def lane_dot(left, right):
    return jnp.sum(left * right, axis=-1, keepdims=True)


def as_bf16(tensor):
    return tensor.astype(jnp.bfloat16).astype(jnp.float32)


def piece_sizes(rows, span):
    even = rows // span
    shift = even // 4 // ROW_TILE * ROW_TILE if span == 4 else 0
    return [even + shift if t in (0, span - 1) else even - shift for t in range(span)]


def needed(source, span):
    return ((0, 3) if source > 0 else ()) + ((1, 2) if source < span - 1 else ())


def returned_to(target, span):
    return ((0, 1) if target > 0 else ()) + ((2, 3) if target < span - 1 else ())


def softmax_weights(scores):
    peak = functools.reduce(jnp.maximum, scores)
    total = functools.reduce(jnp.add, [jnp.exp(score - peak) for score in scores])
    log_total = peak + jnp.log(total)
    return [jnp.exp(score - log_total) for score in scores]


def strided_tile(span, score_scale, queries, keyset, valueset, upstream, last_score, last_grad):
    last = span - 1
    attended, grad_query = [None] * span, [None] * span
    grad_keys, grad_values = [None] * span, [None] * span

    def plus(total, term):
        return term if total is None else total + term

    for p in range(1, span):
        count = min(p + 1, last)
        scores = [lane_dot(queries[p], keyset[j]) * score_scale for j in range(count)]
        grads = [lane_dot(upstream[p], valueset[j]) for j in range(count)]
        if p == last:
            scores.append(last_score)
            grads.append(last_grad)
        weights = softmax_weights(scores)
        rounded_weights = [as_bf16(weight) for weight in weights]
        out, dq = None, None
        for j in range(count):
            out = plus(out, rounded_weights[j] * valueset[j])
            grad_values[j] = plus(grad_values[j], rounded_weights[j] * upstream[p])
        attended[p] = out.astype(jnp.bfloat16)
        if p == last:
            row_dots = functools.reduce(
                jnp.add, [weight * grad for weight, grad in zip(rounded_weights, grads)]
            )
        else:
            row_dots = lane_dot(upstream[p], attended[p].astype(jnp.float32))
        for j in range(count):
            score_grads = as_bf16(weights[j] * (grads[j] - row_dots))
            dq = plus(dq, score_grads * keyset[j])
            grad_keys[j] = plus(grad_keys[j], score_grads * queries[p])
        grad_query[p] = dq * score_scale
    last_weight = rounded_weights[last]
    last_score_grad = as_bf16(weights[last] * (grads[last] - row_dots))
    grad_keys = [tensor if tensor is None else tensor * score_scale for tensor in grad_keys]
    return (attended, grad_query, grad_keys, grad_values), last_weight, last_score_grad


def strided_role(place, span, hop, ins, outs, buffers, sems):
    gathered, results, pair_in, pair_use, pair_out, pair_back = buffers
    in_send, in_recv, out_send, out_recv, own_sem, ps_send, ps_recv, pb_send, pb_recv = sems
    rows, width = ins[0].shape
    sizes = piece_sizes(rows, span)
    starts = [sum(sizes[:t]) for t in range(span)]
    last = span - 1
    size = sizes[place]
    offset = lax.rem(lax.axis_index("seq"), hop)
    chunk_cols = CHUNK_HEADS * HEAD_DIM
    chunks = width // chunk_cols
    heads = width // HEAD_DIM
    score_scale = HEAD_DIM ** (-0.5)
    others = [(place + step) % span for step in range(1, span)]
    mine = pl.ds(starts[place], size)

    def seq_of(member):
        return {"seq": member * hop + offset}

    def rows_of(member):
        return pl.ds(starts[member], sizes[member])

    def remote(src, dst, send, recv, member):
        return pltpu.make_async_remote_copy(
            src_ref=src,
            dst_ref=dst,
            send_sem=send,
            recv_sem=recv,
            device_id=seq_of(member),
            device_id_type=MESH,
        )

    barrier = pltpu.get_barrier_semaphore()
    for member in others:
        pl.semaphore_signal(barrier, 1, device_id=seq_of(member), device_id_type=MESH)
    pl.semaphore_wait(barrier, span - 1)

    own = []
    for i in range(4):
        own.append(
            pltpu.make_async_copy(
                ins[i].at[mine], gathered.at[i, place, pl.ds(0, size)], own_sem.at[i]
            )
        )
        own[-1].start()
    sent = []

    def send_chunk(c):
        cols = pl.ds(c * chunk_cols, chunk_cols)
        for member in others:
            for i in needed(place, span):
                copy = remote(
                    ins[i].at[rows_of(member), cols],
                    gathered.at[i, place, pl.ds(0, sizes[member]), cols],
                    in_send.at[c, member, i],
                    in_recv.at[c, place, i],
                    member,
                )
                copy.start()
                sent.append(copy)

    send_chunk(0)
    lanes = lax.broadcasted_iota(jnp.int32, (ROW_TILE, 128), 1)
    if place == last:

        def pair_body(index, carry):
            row = pl.ds(pl.multiple_of(index * ROW_TILE, ROW_TILE), ROW_TILE)
            kept = jnp.zeros((ROW_TILE, 128), jnp.float32)
            for h in range(heads):
                col = pl.ds(h * HEAD_DIM, HEAD_DIM)
                q, k, v, g = [ref[row, col].astype(jnp.float32) for ref in ins]
                kept = jnp.where(lanes == 2 * h, lane_dot(q, k) * score_scale, kept)
                kept = jnp.where(lanes == 2 * h + 1, lane_dot(g, v), kept)
            pair_in[row, :] = kept
            return carry

        lax.fori_loop(0, rows // ROW_TILE, pair_body, 0)
        for member in others:
            copy = remote(
                pair_in.at[rows_of(member)],
                pair_use.at[pl.ds(0, sizes[member])],
                ps_send.at[member],
                ps_recv.at[0],
                member,
            )
            copy.start()
            sent.append(copy)
        pair_use[pl.ds(0, size), :] = pair_in[mine, :]
    for c in range(1, chunks):
        send_chunk(c)
    for copy in own:
        copy.wait()
    if place != last:
        piece = pair_use.at[pl.ds(0, size)]
        remote(piece, piece, ps_send.at[last], ps_recv.at[0], last).wait_recv()
    tiles = size // ROW_TILE
    for c in range(chunks):
        cols = pl.ds(c * chunk_cols, chunk_cols)
        for member in others:
            for i in needed(member, span):
                piece = gathered.at[i, member, pl.ds(0, size), cols]
                remote(
                    piece, piece, in_send.at[c, member, i], in_recv.at[c, member, i], member
                ).wait_recv()
        pair_out[c] = jnp.zeros(pair_out.shape[1:], jnp.float32)

        def body(index, carry, c=c):
            row = pl.ds(pl.multiple_of(lax.rem(index, tiles) * ROW_TILE, ROW_TILE), ROW_TILE)
            head = index // tiles
            col = pl.ds(pl.multiple_of(c * chunk_cols + head * HEAD_DIM, HEAD_DIM), HEAD_DIM)
            loaded = [
                [
                    gathered[i, j, row, col].astype(jnp.float32) if i in needed(j, span) else None
                    for j in range(span)
                ]
                for i in range(4)
            ]
            pairs = pair_use[row, :]
            lane = 2 * (c * CHUNK_HEADS + head)

            def at_lane(k):
                return jnp.sum(jnp.where(lanes == k, pairs, 0.0), axis=-1, keepdims=True)

            made, weight, grad = strided_tile(
                span, score_scale, *loaded, at_lane(lane), at_lane(lane + 1)
            )
            for j in range(span):
                for i in returned_to(j, span):
                    results[i, j, row, col] = made[i][j].astype(jnp.bfloat16)
            kept = pair_out[c, row, :]
            kept = jnp.where(lanes == 2 * head, weight, kept)
            pair_out[c, row, :] = jnp.where(lanes == 2 * head + 1, grad, kept)
            return carry

        lax.fori_loop(0, tiles * CHUNK_HEADS, body, 0)
        for member in others:
            for i in returned_to(member, span):
                copy = remote(
                    results.at[i, member, pl.ds(0, size), cols],
                    outs[i].at[mine, cols],
                    out_send.at[c, member, i],
                    out_recv.at[c, place, i],
                    member,
                )
                copy.start()
                sent.append(copy)
        if place != last:
            copy = remote(
                pair_out.at[c, pl.ds(0, size)],
                pair_back.at[c, mine],
                pb_send.at[c],
                pb_recv.at[c, place],
                last,
            )
            copy.start()
            sent.append(copy)
        else:
            pair_back[c, mine, :] = pair_out[c, pl.ds(0, size), :]
    for i in returned_to(place, span):
        outs[i][mine, :] = results[i, place, pl.ds(0, size), :]
    big = rows // 4
    big_lanes = lax.broadcasted_iota(jnp.int32, (big, 128), 1)
    for c in range(chunks):
        cols = pl.ds(c * chunk_cols, chunk_cols)
        for member in others:
            for i in returned_to(place, span):
                piece = outs[i].at[rows_of(member), cols]
                remote(
                    piece, piece, out_send.at[c, member, i], out_recv.at[c, member, i], member
                ).wait_recv()
            if place == last:
                piece = pair_back.at[c, rows_of(member)]
                remote(piece, piece, pb_send.at[c], pb_recv.at[c, member], member).wait_recv()
        if place not in (0, last):
            continue

        def close(index, carry, c=c):
            row = pl.ds(pl.multiple_of(lax.rem(index, 4) * big, big), big)
            head = index // 4
            col = pl.ds(pl.multiple_of(c * chunk_cols + head * HEAD_DIM, HEAD_DIM), HEAD_DIM)
            q, k, v, g = [ref[row, col].astype(jnp.float32) for ref in ins]
            if place == last:
                kept = pair_back[c, row, :]
                weight, grad = [
                    jnp.sum(jnp.where(big_lanes == 2 * head + n, kept, 0.0), -1, keepdims=True)
                    for n in range(2)
                ]
                terms = (weight * v, grad * k * score_scale, grad * q * score_scale, weight * g)
            else:
                (weight,) = softmax_weights([lane_dot(q, k) * score_scale])
                out = as_bf16(weight) * v
                row_dots = lane_dot(g, as_bf16(out))
                grad = as_bf16(weight * (lane_dot(g, v) - row_dots))
                terms = (out, grad * k * score_scale, grad * q * score_scale, as_bf16(weight) * g)
            for i in range(4):
                total = terms[i]
                if i in returned_to(place, span):
                    total = total + outs[i][row, col].astype(jnp.float32)
                outs[i][row, col] = total.astype(jnp.bfloat16)
            return carry

        lax.fori_loop(0, 4 * CHUNK_HEADS, close, 0)
    for copy in sent:
        copy.wait_send()


def dot_nt(left, right):
    return lax.dot_general(left, right, (((1,), (1,)), ((), ())), preferred_element_type=jnp.float32)


def dot_nn(left, right):
    return lax.dot_general(left, right, (((1,), (0,)), ((), ())), preferred_element_type=jnp.float32)


def dot_tn(left, right):
    return lax.dot_general(left, right, (((0,), (0,)), ((), ())), preferred_element_type=jnp.float32)


def band_role(ins, outs, halo, held, terms, after, sems):
    halo_send, halo_recv, after_send, after_recv = sems
    query_ref, key_ref, value_ref, grad_ref = ins
    out_ref, dq_ref, dk_ref, dv_ref = outs
    rows, width = query_ref.shape
    heads = width // HEAD_DIM
    blocks = rows // BLOCK
    slab = lax.axis_index("seq")
    slabs = lax.axis_size("seq")
    has_before = slab > 0
    has_after = slab < slabs - 1
    score_scale = HEAD_DIM ** (-0.5)
    before_id = {"seq": jnp.maximum(slab - 1, 0)}
    after_id = {"seq": jnp.minimum(slab + 1, slabs - 1)}

    barrier = pltpu.get_barrier_semaphore()

    @pl.when(has_before)
    def _():
        pl.semaphore_signal(barrier, 1, device_id=before_id, device_id_type=MESH)

    @pl.when(has_after)
    def _():
        pl.semaphore_signal(barrier, 1, device_id=after_id, device_id_type=MESH)

    peers = has_before.astype(jnp.int32) + has_after.astype(jnp.int32)
    pl.semaphore_wait(barrier, peers)

    last_rows = pl.ds(rows - BLOCK, BLOCK)
    halo_copies = [
        pltpu.make_async_remote_copy(
            src_ref=ref.at[last_rows],
            dst_ref=halo.at[i],
            send_sem=halo_send.at[i],
            recv_sem=halo_recv.at[i],
            device_id=after_id,
            device_id_type=MESH,
        )
        for i, ref in enumerate((key_ref, value_ref))
    ]
    after_copies = [
        pltpu.make_async_remote_copy(
            src_ref=terms.at[i],
            dst_ref=after.at[i],
            send_sem=after_send.at[i],
            recv_sem=after_recv.at[i],
            device_id=before_id,
            device_id_type=MESH,
        )
        for i in range(2)
    ]

    @pl.when(has_after)
    def _():
        for copy in halo_copies:
            copy.start()

    row_pos = lax.broadcasted_iota(jnp.int32, (BLOCK, 2 * BLOCK), 0)
    key_pos = lax.broadcasted_iota(jnp.int32, (BLOCK, 2 * BLOCK), 1)
    in_window = (key_pos > row_pos) & (key_pos <= row_pos + BLOCK)
    in_first = in_window & (slab * rows - BLOCK + key_pos >= 0)

    def block_step(block, allowed, h):
        col = pl.ds(pl.multiple_of(h * HEAD_DIM, HEAD_DIM), HEAD_DIM)
        own = pl.ds(block * BLOCK, BLOCK)
        prev = pl.ds((block - 1) * BLOCK, BLOCK)
        if block == 0:
            before_keys, before_values = halo[0, :, col], halo[1, :, col]
        else:
            before_keys, before_values = key_ref[prev, col], value_ref[prev, col]
        keyset = jnp.concatenate([before_keys, key_ref[own, col]], 0)
        valueset = jnp.concatenate([before_values, value_ref[own, col]], 0)
        queries, upstream = query_ref[own, col], grad_ref[own, col]
        scores = jnp.where(allowed, dot_nt(queries, keyset) * score_scale, NEG_FILL)
        peak = jnp.max(scores, axis=-1, keepdims=True)
        log_total = peak + jnp.log(jnp.sum(jnp.exp(scores - peak), axis=-1, keepdims=True))
        weights = jnp.exp(scores - log_total)
        rounded_weights = weights.astype(jnp.bfloat16)
        attended = dot_nn(rounded_weights, valueset).astype(jnp.bfloat16)
        row_dots = lane_dot(upstream.astype(jnp.float32), attended.astype(jnp.float32))
        weight_grads = dot_nt(upstream, valueset)
        score_grads = (weights * (weight_grads - row_dots)).astype(jnp.bfloat16)
        out_ref[own, col] = attended
        dq_ref[own, col] = (dot_nn(score_grads, keyset) * score_scale).astype(jnp.bfloat16)
        key_terms = dot_tn(score_grads, queries) * score_scale
        value_terms = dot_tn(rounded_weights, upstream)
        for i, sums in enumerate((key_terms, value_terms)):
            dst = (dk_ref, dv_ref)[i]
            if block == blocks - 1:
                held[i, block, :, col] = sums[BLOCK:]
            else:
                total = sums[BLOCK:] + held[i, block, :, col]
                dst[own, col] = total.astype(jnp.bfloat16)
            if block > 0:
                held[i, block - 1, :, col] = sums[:BLOCK]
            else:
                terms[i, :, col] = sums[:BLOCK].astype(jnp.bfloat16)

    for block in range(blocks - 1, 0, -1):

        def body(h, carry, block=block):
            block_step(block, in_window, h)
            return carry

        lax.fori_loop(0, heads, body, 0)

    @pl.when(has_before)
    def _():
        for copy in halo_copies:
            copy.wait_recv()

    @pl.when(jnp.logical_not(has_before))
    def _():
        halo[...] = jnp.zeros_like(halo)

    def first_body(h, carry):
        block_step(0, in_first, h)
        return carry

    lax.fori_loop(0, heads, first_body, 0)

    @pl.when(has_before)
    def _():
        for copy in after_copies:
            copy.start()

    @pl.when(has_after)
    def _():
        for copy in after_copies:
            copy.wait_recv()

    @pl.when(jnp.logical_not(has_after))
    def _():
        after[...] = jnp.zeros_like(after)

    for i, dst in enumerate((dk_ref, dv_ref)):
        dst[last_rows, :] = (held[i, blocks - 1] + after[i].astype(jnp.float32)).astype(
            jnp.bfloat16
        )

    @pl.when(has_before)
    def _():
        for copy in after_copies:
            copy.wait_send()

    @pl.when(has_after)
    def _():
        for copy in halo_copies:
            copy.wait_send()


def fused_kernel(span, hop, *refs):
    ins, outs = refs[:4], refs[4:8]
    buffers, (halo, held, terms, after) = refs[8:14], refs[14:18]
    sems = refs[18:]
    is_band = lax.axis_index("head") < lax.axis_size("head") // 2
    place = lax.axis_index("seq") // hop

    @pl.when(is_band)
    def _():
        band_role(ins, outs, halo, held, terms, after, sems[9:])

    for t in range(span):

        @pl.when(jnp.logical_not(is_band) & (place == t))
        def _(t=t):
            strided_role(t, span, hop, ins, outs, buffers, sems[:9])


def place_kernel(*refs):
    made, outs, out_sem = refs[:4], refs[4:8], refs[8]
    gives = [pltpu.make_async_copy(made[i], outs[i], out_sem.at[i]) for i in range(4)]
    for copy in gives:
        copy.start()
    for copy in gives:
        copy.wait()


def placed(made):
    shape, dtype = made[0].shape, made[0].dtype
    return tuple(
        pl.pallas_call(
            place_kernel,
            out_shape=[jax.ShapeDtypeStruct(shape, dtype)] * 4,
            in_specs=[pl.BlockSpec(memory_space=pltpu.VMEM)] * 4,
            out_specs=[pl.BlockSpec(memory_space=pl.ANY)] * 4,
            scratch_shapes=[pltpu.SemaphoreType.DMA((4,))],
        )(*[pltpu.with_memory_space_constraint(part, pltpu.VMEM) for part in made])
    )


def fused_shards(span, hop, *tensors):
    rows, width = tensors[0].shape
    piece = max(piece_sizes(rows, span))
    chunks = width // (CHUNK_HEADS * HEAD_DIM)
    copy_sems = pltpu.SemaphoreType.DMA((chunks, span, 4))
    pair_sems = pltpu.SemaphoreType.DMA((2,))
    vmem = pl.BlockSpec(memory_space=pltpu.VMEM)
    return placed(
        pl.pallas_call(
            functools.partial(fused_kernel, span, hop),
            out_shape=[pltpu.VMEM((rows, width), jnp.bfloat16)] * 4,
            in_specs=[vmem] * 4,
            out_specs=[vmem] * 4,
            scratch_shapes=[
                pltpu.VMEM((4, span, piece, width), jnp.bfloat16),
                pltpu.VMEM((4, span, piece, width), jnp.bfloat16),
                pltpu.VMEM((rows, 128), jnp.float32),
                pltpu.VMEM((piece, 128), jnp.float32),
                pltpu.VMEM((chunks, piece, 128), jnp.float32),
                pltpu.VMEM((chunks, rows, 128), jnp.float32),
                pltpu.VMEM((2, BLOCK, width), jnp.bfloat16),
                pltpu.VMEM((2, rows // BLOCK, BLOCK, width), jnp.float32),
                pltpu.VMEM((2, BLOCK, width), jnp.bfloat16),
                pltpu.VMEM((2, BLOCK, width), jnp.bfloat16),
                copy_sems,
                copy_sems,
                copy_sems,
                copy_sems,
                pltpu.SemaphoreType.DMA((4,)),
                pltpu.SemaphoreType.DMA((span,)),
                pltpu.SemaphoreType.DMA((1,)),
                pltpu.SemaphoreType.DMA((chunks,)),
                pltpu.SemaphoreType.DMA((chunks, span)),
                pair_sems,
                pair_sems,
                pair_sems,
                pair_sems,
            ],
            compiler_params=pltpu.CompilerParams(collective_id=0, has_side_effects=True),
        )(*tensors)
    )


def shards(query_rows, key_rows, value_rows, grad_out):
    rows = query_rows.shape[0]
    hop = STRIDE // rows
    span = lax.axis_size("seq") // hop
    if 2 <= span <= 8 and rows % (span * ROW_TILE) == 0:
        return fused_shards(span, hop, query_rows, key_rows, value_rows, grad_out)
    return swapped_shards(query_rows, key_rows, value_rows, grad_out)


def solution(mesh):
    return jax.shard_map(
        shards,
        mesh=mesh,
        in_specs=(P("seq", "head"), P("seq", "head"), P("seq", "head"), P("seq", "head")),
        out_specs=(P("seq", "head"), P("seq", "head"), P("seq", "head"), P("seq", "head")),
        check_vma=False,
    )
```
